128 devices in a mesh: cam: 4 (over y), tile: 32 (over z, x, core).
Axes of the slice: x: 4, y: 4, z: 4, core: 2. Of those that a mesh axis runs over, the one named last changes fastest.
Arguments:
- splat_params: float32 [59, 2097152], P(None, ('cam', 'tile'))
- first_moment: float32 [59, 2097152], P(None, ('cam', 'tile')), may hold values from -6 to 6
- second_moment: float32 [59, 2097152], P(None, ('cam', 'tile')), may hold values from 0.05 to 2
- camera_turn: float32 [4, 3], replicated, may hold values from -0.004 to 0.004
- camera_shift: float32 [4, 3], replicated, may hold values from -0.05 to 0.05
- fetch_table: int32 [128, 128, 128], P(('cam', 'tile')), may hold values from 0 to 16383, as said below
- tile_lists: int32 [4, 1024, 256], P('cam', 'tile'), may hold values from 0 to 16383, as said below
- tile_counts: int32 [4, 1024], P('cam', 'tile'), may hold values from 128 to 256, as said below
- tile_ids: int32 [4, 1024], P('cam', 'tile'), may hold values from 0 to 1023, as said below
- target_image: float32 [3, 4, 1024, 256], P(None, 'cam', 'tile'), may hold values from 0 to 1
Outputs:
- updated_params: float32 [59, 2097152], P(None, ('cam', 'tile'))
- updated_first: float32 [59, 2097152], P(None, ('cam', 'tile'))
- updated_second: float32 [59, 2097152], P(None, ('cam', 'tile'))
- rendered: float32 [3, 4, 1024, 256], P(None, 'cam', 'tile')
The draws below stay inside these ranges and needn't reach their ends.
Inputs may be any that keep to these rules, and one draw needn't show every extreme that they name: `fetch_table`: for each source device, its entries over all rendering devices and slots name every one of its 16384 Gaussians exactly once. `tile_lists`: entries are slot numbers of the rendering device; no slot is named twice among all entries of the 32 tiles of one device. Live entries are in front-to-back order, and a Gaussian is named by at most one live entry of all lists. `tile_counts`: in every device one tile's list is full. `tile_ids`: for each camera, a permutation of its 1024 tile numbers.
All inputs are finite; a program needn't handle non-finite values.
Results may differ from the reference program's by a relative error of at most 0.0003.
Values sent between devices are 32-bit elements; how exact they have to be, the bound alone decides.
A program may use at most 192 MiB of HBM per device.

```python
import math
import jax
import jax.numpy as jnp
from jax import lax

TILE_DEV = 32
LIST = 256
TILE_PX = 16
GRID = 32
SH_COEF = 48
CAMS = 4
TILES_CAM = 1024
G_DEV = 16384
CAP = 128
GAUSS = 2097152
N_TILE = 32
DEVICES = 128


def plan_tables(key):
    base = jax.random.fold_in(key, 101)
    parts_keys = jax.random.split(base, 5)
    tile_perm = jax.vmap(lambda sub_key: jax.random.permutation(sub_key, TILES_CAM))(jax.random.split(parts_keys[0], CAMS))
    counts = jax.random.randint(parts_keys[1], (DEVICES * TILE_DEV,), LIST // 2, LIST + 1)
    full_at = jax.random.randint(parts_keys[2], (DEVICES,), 0, TILE_DEV)
    counts = counts.at[jnp.arange(DEVICES) * TILE_DEV + full_at].set(LIST)
    slot_perm = jax.vmap(lambda sub_key: jax.random.permutation(sub_key, DEVICES * CAP))(jax.random.split(parts_keys[3], DEVICES))
    lists_all = slot_perm[:, :TILE_DEV * LIST].reshape(CAMS, TILES_CAM, LIST)
    owner_perm = jax.vmap(lambda sub_key: jax.random.permutation(sub_key, G_DEV))(jax.random.split(parts_keys[4], DEVICES))
    table = jnp.transpose(owner_perm.reshape(DEVICES, DEVICES, CAP), (1, 0, 2))
    return (tile_perm.astype(jnp.int32), counts.reshape(CAMS, TILES_CAM).astype(jnp.int32), lists_all.astype(jnp.int32), table.astype(jnp.int32))


def draw_fetch_table(key, part):
    return plan_tables(key)[3]


def draw_tile_lists(key, part):
    return plan_tables(key)[2]


def draw_tile_counts(key, part):
    return plan_tables(key)[1]


def draw_tile_ids(key, part):
    return plan_tables(key)[0]


def draw_splat_params(key, part):
    tile_perm, counts, lists_all, table = plan_tables(key)
    total_count = G_DEV * DEVICES
    by_device = lists_all.reshape(DEVICES, TILE_DEV, LIST)
    source = by_device // CAP
    within = by_device % CAP
    owner = jnp.arange(DEVICES)[:, None, None]
    gaussian = source * G_DEV + table[owner, source, within]
    entry = jnp.broadcast_to(jnp.arange(LIST)[None, None, :], by_device.shape)
    live = entry < counts.reshape(DEVICES, TILE_DEV)[:, :, None]
    where_to = jnp.where(live, gaussian, total_count).reshape(-1)
    tile_of = jnp.broadcast_to(tile_perm.reshape(DEVICES, TILE_DEV)[:, :, None], by_device.shape).reshape(-1)
    cam_of = jnp.broadcast_to((jnp.arange(DEVICES) // N_TILE)[:, None, None], by_device.shape).reshape(-1)
    draw_keys = jax.random.split(jax.random.fold_in(key, 202), 12)
    home_tile = jax.random.randint(draw_keys[0], (total_count,), 0, TILES_CAM)
    home_cam = jax.random.randint(draw_keys[1], (total_count,), 0, CAMS)
    home_rank = jax.random.randint(draw_keys[2], (total_count,), 0, LIST)
    home_tile = home_tile.at[where_to].set(tile_of, mode='drop')
    home_cam = home_cam.at[where_to].set(cam_of, mode='drop')
    home_rank = home_rank.at[where_to].set(entry.reshape(-1), mode='drop')
    across = jax.random.uniform(draw_keys[3], (total_count,)) * TILE_PX
    downward = jax.random.uniform(draw_keys[4], (total_count,)) * TILE_PX
    pixel_x = (home_tile % GRID * TILE_PX).astype(jnp.float32) + across
    pixel_y = (home_tile // GRID * TILE_PX).astype(jnp.float32) + downward
    depth = 8.0 + 4.0 * (home_rank.astype(jnp.float32) + jax.random.uniform(draw_keys[5], (total_count,))) / LIST
    world_x = (pixel_x - 256.0) * depth / 512.0 + 20.0 * home_cam.astype(jnp.float32)
    world_y = (pixel_y - 256.0) * depth / 512.0
    quat_w = jax.random.uniform(draw_keys[6], (1, total_count), minval=0.6, maxval=1.4)
    log_scale = jax.random.uniform(draw_keys[7], (3, total_count), minval=math.log(0.03), maxval=math.log(0.08))
    quat_rest = jax.random.uniform(draw_keys[8], (3, total_count), minval=-0.5, maxval=0.5)
    opacity_raw = jax.random.uniform(draw_keys[9], (1, total_count), minval=-6.0, maxval=-1.0)
    colour_base = jax.random.normal(draw_keys[10], (3, total_count))
    colour_rest = 0.2 * jax.random.normal(draw_keys[11], (SH_COEF - 3, total_count))
    return jnp.concatenate([world_x[None], world_y[None], depth[None], log_scale, quat_w, quat_rest, opacity_raw, colour_base, colour_rest], axis=0).astype(jnp.float32)


def levels(stream_key, dims, pieces, low, largest):
    factor_of = 1.0
    for dim, parts in pieces:
        steps = jax.random.uniform(jax.random.fold_in(jax.random.fold_in(stream_key, 6), dim), (parts,), jnp.float32, low / len(pieces), largest / len(pieces))
        factor_of = factor_of * jnp.repeat(jnp.exp(steps), dims[dim] // parts).reshape((-1,) + (1,) * (len(dims) - 1 - dim))
    return factor_of


def normal_values(own_key, extent, width, most, pieces=(), kind=jnp.bfloat16):
    values = width * jax.random.normal(own_key, extent, jnp.float32)
    if pieces:
        values = values * levels(own_key, extent, pieces, -0.22, 0.18)
    return jnp.clip(values, -most, most).astype(kind)


def setup_inputs(seed: int = 0) -> dict:
    streams_of = jax.random.split(jax.random.key(seed), 11)
    return {
        "splat_params": draw_splat_params(jax.random.fold_in(streams_of[10], 71), 0),
        "first_moment": normal_values(streams_of[1], (11 + SH_COEF, GAUSS), 1.0, 6.0, ((1, 128),), jnp.float32),
        "second_moment": jnp.clip(jnp.exp(math.log(2.0) - 3.6888794 * jax.random.uniform(streams_of[2], (11 + SH_COEF, GAUSS), jnp.float32) ** levels(streams_of[2], (11 + SH_COEF, GAUSS), ((1, 128),), -0.2, 0.2)), 0.05, 2.0),
        "camera_turn": jnp.clip(jax.random.uniform(streams_of[3], (CAMS, 3), jnp.float32, -0.004, 0.004), -0.004, 0.004),
        "camera_shift": jnp.clip(jax.random.uniform(streams_of[4], (CAMS, 3), jnp.float32, -0.05, 0.05), -0.05, 0.05),
        "fetch_table": draw_fetch_table(jax.random.fold_in(streams_of[10], 71), 0),
        "tile_lists": draw_tile_lists(jax.random.fold_in(streams_of[10], 71), 0),
        "tile_counts": draw_tile_counts(jax.random.fold_in(streams_of[10], 71), 0),
        "tile_ids": draw_tile_ids(jax.random.fold_in(streams_of[10], 71), 0),
        "target_image": jnp.clip(1.0 * jax.random.uniform(streams_of[9], (3, CAMS, TILES_CAM, TILE_PX * TILE_PX), jnp.float32) ** levels(streams_of[9], (3, CAMS, TILES_CAM, TILE_PX * TILE_PX), ((1, 4), (2, 32)), -0.2, 0.2), 0.0, 1.0),
    }


FOCAL = 512.0
CENTRE = 256.0
EYE_GAP = 20.0
DILATION = 0.3
SH_ZERO = 0.28209479177387814
SH_ONE = 0.4886025119029199
SH_TWO = (1.0925484305920792, -1.0925484305920792, 0.31539156525252005, -1.0925484305920792, 0.5462742152960396)
SH_THREE = (-0.5900435899266435, 2.890611442640554, -0.4570457994644658, 0.3731763325901154, -0.4570457994644658, 1.445305721320277, -0.5900435899266435)
BETA_ONE = 0.9
BETA_TWO = 0.999
BIAS_ONE = 1.0 - math.exp(2000.0 * math.log(0.9))
BIAS_TWO = 1.0 - math.exp(2000.0 * math.log(0.999))
ADAM_EPS = 1e-08

def harmonics(dir_x, dir_y, dir_z):
    sq_x = dir_x * dir_x
    sq_y = dir_y * dir_y
    sq_z = dir_z * dir_z
    return [SH_ZERO * jnp.ones_like(dir_x), -SH_ONE * dir_y, SH_ONE * dir_z, -SH_ONE * dir_x, SH_TWO[0] * dir_x * dir_y, SH_TWO[1] * dir_y * dir_z, SH_TWO[2] * (2.0 * sq_z - sq_x - sq_y), SH_TWO[3] * dir_x * dir_z, SH_TWO[4] * (sq_x - sq_y), SH_THREE[0] * dir_y * (3.0 * sq_x - sq_y), SH_THREE[1] * dir_x * dir_y * dir_z, SH_THREE[2] * dir_y * (4.0 * sq_z - sq_x - sq_y), SH_THREE[3] * dir_z * (2.0 * sq_z - 3.0 * sq_x - 3.0 * sq_y), SH_THREE[4] * dir_x * (4.0 * sq_z - sq_x - sq_y), SH_THREE[5] * dir_z * (sq_x - sq_y), SH_THREE[6] * dir_x * (sq_x - 3.0 * sq_y)]

def quat_matrix(quat_w, quat_x, quat_y, quat_z):
    return [[1.0 - 2.0 * (quat_y * quat_y + quat_z * quat_z), 2.0 * (quat_x * quat_y - quat_w * quat_z), 2.0 * (quat_x * quat_z + quat_w * quat_y)], [2.0 * (quat_x * quat_y + quat_w * quat_z), 1.0 - 2.0 * (quat_x * quat_x + quat_z * quat_z), 2.0 * (quat_y * quat_z - quat_w * quat_x)], [2.0 * (quat_x * quat_z - quat_w * quat_y), 2.0 * (quat_y * quat_z + quat_w * quat_x), 1.0 - 2.0 * (quat_x * quat_x + quat_y * quat_y)]]

def project(params, cam_quat, eye_pos):
    scales = [jnp.exp(params[3 + i]) for i in range(3)]
    norm_quat = jnp.sqrt(params[6] * params[6] + params[7] * params[7] + params[8] * params[8] + params[9] * params[9])
    rotation = quat_matrix(params[6] / norm_quat, params[7] / norm_quat, params[8] / norm_quat, params[9] / norm_quat)
    camera = quat_matrix(cam_quat[0], cam_quat[1], cam_quat[2], cam_quat[3])
    relative = [params[i] - eye_pos[i] for i in range(3)]
    in_view = [camera[i][0] * relative[0] + camera[i][1] * relative[1] + camera[i][2] * relative[2] for i in range(3)]
    inv_depth = 1.0 / in_view[2]
    screen_x = FOCAL * in_view[0] * inv_depth + CENTRE
    screen_y = FOCAL * in_view[1] * inv_depth + CENTRE
    axes_cam = [[(camera[i][0] * rotation[0][k] + camera[i][1] * rotation[1][k] + camera[i][2] * rotation[2][k]) * scales[k] for k in range(3)] for i in range(3)]
    slope_x = FOCAL * in_view[0] * inv_depth * inv_depth
    slope_y = FOCAL * in_view[1] * inv_depth * inv_depth
    row_x = [FOCAL * inv_depth * axes_cam[0][k] - slope_x * axes_cam[2][k] for k in range(3)]
    row_y = [FOCAL * inv_depth * axes_cam[1][k] - slope_y * axes_cam[2][k] for k in range(3)]
    cov_xx = row_x[0] * row_x[0] + row_x[1] * row_x[1] + row_x[2] * row_x[2] + DILATION
    cov_xy = row_x[0] * row_y[0] + row_x[1] * row_y[1] + row_x[2] * row_y[2]
    cov_yy = row_y[0] * row_y[0] + row_y[1] * row_y[1] + row_y[2] * row_y[2] + DILATION
    determinant = cov_xx * cov_yy - cov_xy * cov_xy
    distance = jnp.sqrt(relative[0] * relative[0] + relative[1] * relative[1] + relative[2] * relative[2])
    basis = harmonics(relative[0] / distance, relative[1] / distance, relative[2] / distance)
    colours = []
    for channel in range(3):
        total = basis[0] * params[11 + channel]
        for k in range(1, 16):
            total = total + basis[k] * params[11 + 3 * k + channel]
        colours.append(jnp.maximum(total + 0.5, 0.0))
    opacity = jax.nn.sigmoid(params[10])
    return jnp.stack([screen_x, screen_y, cov_yy / determinant, -cov_xy / determinant, cov_xx / determinant, colours[0], colours[1], colours[2], opacity])

def camera_quats(camera_turn):
    norm_turn = jnp.sqrt(1.0 + lax.optimization_barrier(jnp.sum(camera_turn * camera_turn, axis=1, keepdims=True)))
    return jnp.concatenate([1.0 / norm_turn, camera_turn / norm_turn], axis=1)

def camera_eyes(camera_shift):
    survey = EYE_GAP * jnp.arange(camera_shift.shape[0]).astype(jnp.float32)
    return jnp.stack([survey + camera_shift[:, 0], camera_shift[:, 1], camera_shift[:, 2]], axis=1)

def pixel_centres(tile_numbers):
    pixel = jnp.arange(TILE_PX * TILE_PX)
    centre_x = (tile_numbers % GRID * TILE_PX)[:, None] + (pixel % TILE_PX)[None, :]
    centre_y = (tile_numbers // GRID * TILE_PX)[:, None] + (pixel // TILE_PX)[None, :]
    return (centre_x.astype(jnp.float32) + 0.5, centre_y.astype(jnp.float32) + 0.5)

def composite(records, counts, tile_numbers, prefix):
    centre_x, centre_y = pixel_centres(tile_numbers)
    offset_x = centre_x[:, :, None] - records[0][:, None, :]
    offset_y = centre_y[:, :, None] - records[1][:, None, :]
    exponent = -0.5 * (records[2][:, None, :] * offset_x * offset_x + records[4][:, None, :] * offset_y * offset_y) - records[3][:, None, :] * offset_x * offset_y
    live = (jnp.arange(records.shape[2])[None, :] < counts[:, None]).astype(jnp.float32)
    alphas = records[8][:, None, :] * live[:, None, :] * jnp.exp(exponent)
    log_keep = jnp.log1p(-alphas)
    weights = jnp.exp(prefix(log_keep)) * alphas
    return jnp.einsum('bpk,cbk->cbp', weights, records[5:8], precision=lax.Precision.HIGHEST)

def before_sum(log_keep):
    inclusive = jnp.cumsum(log_keep, axis=2)
    return jnp.concatenate([jnp.zeros_like(inclusive[:, :, :1]), inclusive[:, :, :-1]], axis=2)

def adam(params, gradient, moment_one, moment_two):
    row_index = jnp.arange(params.shape[0])[:, None]
    step_sizes = jnp.where(row_index < 3, 0.00016, jnp.where(row_index < 6, 0.005, jnp.where(row_index < 10, 0.001, jnp.where(row_index < 11, 0.025, jnp.where(row_index < 14, 0.0025, 0.000125)))))
    new_first = BETA_ONE * moment_one + (1.0 - BETA_ONE) * gradient
    new_second = BETA_TWO * moment_two + (1.0 - BETA_TWO) * gradient * gradient
    new_params = params - step_sizes * (new_first / BIAS_ONE) / (jnp.sqrt(new_second / BIAS_TWO) + ADAM_EPS)
    return (new_params, new_first, new_second)

def reference(splat_params, first_moment, second_moment, camera_turn, camera_shift, fetch_table, tile_lists, tile_counts, tile_ids, target_image):
    cam_quats = camera_quats(camera_turn)
    cam_eyes = camera_eyes(camera_shift)
    owner = (jnp.arange(CAMS)[:, None] * N_TILE + jnp.arange(TILES_CAM)[None, :] // TILE_DEV).astype(jnp.int32)
    source = (tile_lists // CAP).astype(jnp.int32)
    within = (tile_lists % CAP).astype(jnp.int32)
    gaussian = (source * G_DEV + fetch_table[owner[:, :, None], source, within]).astype(jnp.int32).reshape(-1)
    viewer = jnp.broadcast_to(jnp.arange(CAMS)[:, None, None], tile_lists.shape).reshape(-1)
    view_quat = jnp.transpose(cam_quats[viewer])
    view_eye = jnp.transpose(cam_eyes[viewer])

    def records_of(params):
        return project(jnp.take(params, gaussian, axis=1), view_quat, view_eye)
    records, pull_back = jax.vjp(records_of, splat_params)
    groups = CAMS * TILES_CAM // TILE_DEV
    pixels = TILE_PX * TILE_PX
    rec_blocks = jnp.moveaxis(records.reshape(9, groups, TILE_DEV, LIST), 1, 0)
    count_blocks = tile_counts.reshape(groups, TILE_DEV)
    id_blocks = tile_ids.reshape(groups, TILE_DEV)
    goal_blocks = jnp.moveaxis(target_image.reshape(3, groups, TILE_DEV, pixels), 1, 0)

    def tile_step(unused, block_in):
        block_rec, block_count, block_ids, block_goal = block_in
        painted, pull_tiles = jax.vjp(lambda block_records: composite(block_records, block_count, block_ids, before_sum), block_rec)
        rec_grad, = pull_tiles(painted - block_goal)
        return (unused, (painted, rec_grad))
    _, (painted, rec_grads) = lax.scan(tile_step, jnp.zeros((), jnp.float32), (rec_blocks, count_blocks, id_blocks, goal_blocks))
    rendered = jnp.moveaxis(painted, 0, 1).reshape(3, CAMS, TILES_CAM, pixels)
    gradient, = pull_back(jnp.moveaxis(rec_grads, 0, 1).reshape(9, -1))
    updated_params, updated_first, updated_second = adam(splat_params, gradient, first_moment, second_moment)
    return (updated_params, updated_first, updated_second, rendered)
```

```python
import math

import jax
import jax.numpy as jnp
from jax import lax
from jax.experimental import pallas as pl
from jax.experimental.pallas import tpu as pltpu
from jax.sharding import PartitionSpec as P

TILE_PX = 16
GRID = 32


FOCAL = 512.0
CENTRE = 256.0
EYE_GAP = 20.0
DILATION = 0.3
SH_ZERO = 0.28209479177387814
SH_ONE = 0.4886025119029199
SH_TWO = (
    1.0925484305920792,
    -1.0925484305920792,
    0.31539156525252005,
    -1.0925484305920792,
    0.5462742152960396,
)
SH_THREE = (
    -0.5900435899266435,
    2.890611442640554,
    -0.4570457994644658,
    0.3731763325901154,
    -0.4570457994644658,
    1.445305721320277,
    -0.5900435899266435,
)
BETA_ONE = 0.9
BETA_TWO = 0.999
BIAS_ONE = 1.0 - math.exp(2000.0 * math.log(0.9))
BIAS_TWO = 1.0 - math.exp(2000.0 * math.log(0.999))
ADAM_EPS = 1e-08


def harmonics(dir_x, dir_y, dir_z):
    sq_x = dir_x * dir_x
    sq_y = dir_y * dir_y
    sq_z = dir_z * dir_z
    return [
        SH_ZERO * jnp.ones_like(dir_x),
        -SH_ONE * dir_y,
        SH_ONE * dir_z,
        -SH_ONE * dir_x,
        SH_TWO[0] * dir_x * dir_y,
        SH_TWO[1] * dir_y * dir_z,
        SH_TWO[2] * (2.0 * sq_z - sq_x - sq_y),
        SH_TWO[3] * dir_x * dir_z,
        SH_TWO[4] * (sq_x - sq_y),
        SH_THREE[0] * dir_y * (3.0 * sq_x - sq_y),
        SH_THREE[1] * dir_x * dir_y * dir_z,
        SH_THREE[2] * dir_y * (4.0 * sq_z - sq_x - sq_y),
        SH_THREE[3] * dir_z * (2.0 * sq_z - 3.0 * sq_x - 3.0 * sq_y),
        SH_THREE[4] * dir_x * (4.0 * sq_z - sq_x - sq_y),
        SH_THREE[5] * dir_z * (sq_x - sq_y),
        SH_THREE[6] * dir_x * (sq_x - 3.0 * sq_y),
    ]


def quat_matrix(quat_w, quat_x, quat_y, quat_z):
    return [
        [
            1.0 - 2.0 * (quat_y * quat_y + quat_z * quat_z),
            2.0 * (quat_x * quat_y - quat_w * quat_z),
            2.0 * (quat_x * quat_z + quat_w * quat_y),
        ],
        [
            2.0 * (quat_x * quat_y + quat_w * quat_z),
            1.0 - 2.0 * (quat_x * quat_x + quat_z * quat_z),
            2.0 * (quat_y * quat_z - quat_w * quat_x),
        ],
        [
            2.0 * (quat_x * quat_z - quat_w * quat_y),
            2.0 * (quat_y * quat_z + quat_w * quat_x),
            1.0 - 2.0 * (quat_x * quat_x + quat_y * quat_y),
        ],
    ]

LOG2E = math.log2(math.e)
HALF = 64
WIDE = 256
LANES = 128
BIG = 3e38
DEAD = -1e4
KEEP_MIN = 2.0**-24
BF = jnp.bfloat16
F32 = jnp.float32


def project(params, camera, eye_pos):
    scales = [jnp.exp(params[3 + i]) for i in range(3)]
    norm_quat = jnp.sqrt(
        params[6] * params[6]
        + params[7] * params[7]
        + params[8] * params[8]
        + params[9] * params[9]
    )
    rotation = quat_matrix(
        params[6] / norm_quat, params[7] / norm_quat, params[8] / norm_quat, params[9] / norm_quat
    )
    relative = [params[i] - eye_pos[i] for i in range(3)]
    in_view = [
        camera[i][0] * relative[0] + camera[i][1] * relative[1] + camera[i][2] * relative[2]
        for i in range(3)
    ]
    inv_depth = 1.0 / in_view[2]
    screen_x = FOCAL * in_view[0] * inv_depth + CENTRE
    screen_y = FOCAL * in_view[1] * inv_depth + CENTRE
    axes_cam = [
        [
            (
                camera[i][0] * rotation[0][k]
                + camera[i][1] * rotation[1][k]
                + camera[i][2] * rotation[2][k]
            )
            * scales[k]
            for k in range(3)
        ]
        for i in range(3)
    ]
    slope_x = FOCAL * in_view[0] * inv_depth * inv_depth
    slope_y = FOCAL * in_view[1] * inv_depth * inv_depth
    row_x = [FOCAL * inv_depth * axes_cam[0][k] - slope_x * axes_cam[2][k] for k in range(3)]
    row_y = [FOCAL * inv_depth * axes_cam[1][k] - slope_y * axes_cam[2][k] for k in range(3)]
    cov_xx = row_x[0] * row_x[0] + row_x[1] * row_x[1] + row_x[2] * row_x[2] + DILATION
    cov_xy = row_x[0] * row_y[0] + row_x[1] * row_y[1] + row_x[2] * row_y[2]
    cov_yy = row_y[0] * row_y[0] + row_y[1] * row_y[1] + row_y[2] * row_y[2] + DILATION
    inv_det = 1.0 / (cov_xx * cov_yy - cov_xy * cov_xy)
    inv_dist = 1.0 / jnp.sqrt(
        relative[0] * relative[0] + relative[1] * relative[1] + relative[2] * relative[2]
    )
    basis = harmonics(relative[0] * inv_dist, relative[1] * inv_dist, relative[2] * inv_dist)
    colours = []
    for channel in range(3):
        total = basis[0] * params[11 + channel]
        for k in range(1, 16):
            total = total + basis[k] * params[11 + 3 * k + channel]
        colours.append(jnp.maximum(total + 0.5, 0.0))
    return [
        screen_x,
        screen_y,
        cov_yy * inv_det,
        -cov_xy * inv_det,
        cov_xx * inv_det,
        colours[0],
        colours[1],
        colours[2],
    ]


def camera_of(turn_ref, shift_ref, cam, shape):
    turn = [jnp.full(shape, turn_ref[cam, i], F32) for i in range(3)]
    norm = jnp.sqrt(1.0 + (turn[0] * turn[0] + turn[1] * turn[1] + turn[2] * turn[2]))
    matrix = quat_matrix(1.0 / norm, turn[0] / norm, turn[1] / norm, turn[2] / norm)
    eye = [jnp.full(shape, shift_ref[cam, i], F32) for i in range(3)]
    eye[0] = EYE_GAP * cam + eye[0]
    return matrix, eye


def dense_rows(ref, columns):
    rows = []
    total = ref.shape[0]
    for start in range(0, total, 8):
        size = min(8, total - start)
        block = ref[start : start + size, :].reshape(size, columns // LANES, LANES)
        rows.extend(block[r] for r in range(size))
    return rows


def two_parts(value):
    high = value.astype(BF)
    return high, (value - high.astype(F32)).astype(BF)


def nt_dot(lhs, rhs):
    return lax.dot_general(lhs, rhs, (((1,), (1,)), ((), ())), preferred_element_type=F32)


def tn_dot(lhs, rhs):
    return lax.dot_general(lhs, rhs, (((0,), (0,)), ((), ())), preferred_element_type=F32)


def nn_dot(lhs, rhs):
    return lax.dot_general(lhs, rhs, (((1,), (0,)), ((), ())), preferred_element_type=F32)


def one_hots(index):
    count = index.shape[1]
    wide = (index >> 13) * LANES + (index & 127)
    narrow = (index >> 7) & 63
    pick = lax.broadcasted_iota(jnp.int32, (WIDE, count), 0) == wide
    mask = lax.broadcasted_iota(jnp.int32, (HALF, count), 0) == narrow
    return jnp.where(pick, 1.0, 0.0).astype(BF), jnp.where(mask, 1.0, 0.0)


def pick_from(table, low_table, index):
    pick, mask = one_hots(index)
    spread = nn_dot(table, jnp.concatenate([pick, pick], axis=0))
    extra = nn_dot(low_table, pick)
    picked = []
    for r in range(9):
        part = spread[r * HALF : (r + 1) * HALF]
        if r < 2:
            part = part + extra[r * HALF : (r + 1) * HALF]
        picked.append(jnp.sum(part * mask, axis=0, keepdims=True))
    return picked


def put_into(rows, index):
    pick, mask = one_hots(index)
    mask = mask.astype(BF)
    parts = [two_parts(row) for row in rows]
    high = jnp.concatenate([mask * part[0] for part in parts], axis=0)
    low = jnp.concatenate([mask * part[1] for part in parts], axis=0)
    return nt_dot(jnp.concatenate([high, low], axis=1), jnp.concatenate([pick, pick], axis=1))


def records_kernel(turn_ref, shift_ref, left_ref, right_ref, table_ref, low_ref):
    columns = left_ref.shape[1]
    rows = columns // LANES
    for half, ref in enumerate((left_ref, right_ref)):
        params = dense_rows(ref, columns)
        opacity = jax.nn.sigmoid(params[10])
        for cam in range(4):
            matrix, eye = camera_of(turn_ref, shift_ref, cam, (rows, LANES))
            record = project(params, matrix, eye) + [opacity]
            for r, value in enumerate(record):
                value = jnp.where(value == value, jnp.clip(value, -BIG, BIG), 0.0)
                high, mid = two_parts(value)
                at = half * LANES
                table_ref[cam, r, :, at : at + LANES] = high
                table_ref[cam, r, :, WIDE + at : WIDE + at + LANES] = mid
                if r < 2:
                    low = (value - high.astype(F32)) - mid.astype(F32)
                    low_ref[cam, r, :, at : at + LANES] = low.astype(BF)


def project_all(splat_params, camera_turn, camera_shift):
    rows_in, own_count = splat_params.shape
    columns = 2048
    steps = own_count // columns // 2
    rows = columns // LANES
    return pl.pallas_call(
        records_kernel,
        grid=(steps,),
        in_specs=[
            pl.BlockSpec(memory_space=pltpu.SMEM),
            pl.BlockSpec(memory_space=pltpu.SMEM),
            pl.BlockSpec((rows_in, columns), lambda i: (0, i)),
            pl.BlockSpec((rows_in, columns), lambda i: (0, i + steps)),
        ],
        out_specs=[
            pl.BlockSpec((4, 9, rows, 2 * WIDE), lambda i: (0, 0, i, 0)),
            pl.BlockSpec((4, 2, rows, WIDE), lambda i: (0, 0, i, 0)),
        ],
        out_shape=[
            jax.ShapeDtypeStruct((4, 9, HALF, 2 * WIDE), BF),
            jax.ShapeDtypeStruct((4, 2, HALF, WIDE), BF),
        ],
        compiler_params=pltpu.CompilerParams(vmem_limit_bytes=48 << 20),
        name="project_all",
    )(camera_turn, camera_shift, splat_params, splat_params)


def pair_of(ref, step):
    return jnp.concatenate([ref[pl.ds(2 * step, 1), :], ref[pl.ds(2 * step + 1, 1), :]], axis=1)


def answer_kernel(wanted_ref, table_ref, low_ref, out_ref):
    steps = wanted_ref.shape[0] // 2
    per_cam = steps // 4

    def body(step, carry):
        cam = step // per_cam
        picked = pick_from(
            table_ref[cam].reshape(9 * HALF, 2 * WIDE),
            low_ref[cam].reshape(2 * HALF, WIDE),
            pair_of(wanted_ref, step),
        )
        block = jnp.concatenate(picked, axis=0)
        out_ref[2 * step, 0:9, :] = block[:, :LANES]
        out_ref[2 * step + 1, 0:9, :] = block[:, LANES:]
        return carry

    lax.fori_loop(0, steps, body, 0, unroll=2)


def answer(wanted, table, low):
    devices, capacity = wanted.shape
    return pl.pallas_call(
        answer_kernel,
        in_specs=[pl.BlockSpec(memory_space=pltpu.VMEM)] * 3,
        out_specs=pl.BlockSpec(memory_space=pltpu.VMEM),
        out_shape=jax.ShapeDtypeStruct((devices, 16, capacity), F32),
        compiler_params=pltpu.CompilerParams(vmem_limit_bytes=48 << 20),
        name="answer",
    )(wanted, table, low)


def render_kernel(
    counts_ref, ids_ref, got_ref, lists_ref, goal_ref, image_ref, grads_ref,
    table_ref, low_ref, before_ref, after_ref, total_ref,
):
    tiles, entries = lists_ref.shape
    pixels = goal_ref.shape[2]

    for h in range(2):
        for r in range(9):
            value = jnp.concatenate(
                [got_ref[pl.ds((h * HALF + i) * 16 + r, 8, stride=16), :] for i in range(0, HALF, 8)], axis=0
            )
            high, mid = two_parts(value)
            table_ref[r * HALF : (r + 1) * HALF, h * LANES : (h + 1) * LANES] = high
            table_ref[r * HALF : (r + 1) * HALF, WIDE + h * LANES : WIDE + (h + 1) * LANES] = mid
            if r < 2:
                low = (value - high.astype(F32)) - mid.astype(F32)
                low_ref[r * HALF : (r + 1) * HALF, h * LANES : (h + 1) * LANES] = low.astype(BF)
    row = lax.broadcasted_iota(jnp.int32, (entries, entries), 0)
    col = lax.broadcasted_iota(jnp.int32, (entries, entries), 1)
    before_ref[...] = jnp.where(row < col, 1.0, 0.0).astype(BF)
    after_ref[...] = jnp.where(row > col, 1.0, 0.0).astype(BF)
    total_ref[...] = jnp.zeros_like(total_ref)

    def tile_step(tile):
        index = lists_ref[pl.ds(tile, 1), :]
        live = lax.broadcasted_iota(jnp.int32, (1, entries), 1) < counts_ref[0, tile]
        number = ids_ref[0, tile]
        origin_x = ((number & 31) * TILE_PX + TILE_PX // 2).astype(F32)
        origin_y = ((number >> 5) * TILE_PX + TILE_PX // 2).astype(F32)
        rec = pick_from(table_ref[...], low_ref[...], index)
        rec_u = jnp.where(live, rec[0] - origin_x, 0.0)
        rec_v = jnp.where(live, rec[1] - origin_y, 0.0)
        con_a = jnp.where(live, rec[2], 0.0)
        con_b = jnp.where(live, rec[3], 0.0)
        con_c = jnp.where(live, rec[4], 0.0)
        log_o = jnp.where(live, jnp.maximum(jnp.log(rec[8]) * LOG2E, DEAD), DEAD)
        colours = rec[5:8]

        spot = lax.broadcasted_iota(jnp.int32, (TILE_PX, entries), 0).astype(F32) - 7.5
        off_x = spot - rec_u
        off_y = spot - rec_v
        part_x = (-0.5 * LOG2E) * con_a * off_x * off_x + log_o
        cross = (-LOG2E) * con_b * off_x
        part_y = (-0.5 * LOG2E) * con_c * off_y * off_y
        power = jnp.concatenate(
            [part_x + (cross * off_y[y : y + 1] + part_y[y : y + 1]) for y in range(TILE_PX)], axis=0
        )
        alphas = jnp.exp2(power)
        log_keep = jnp.log(jnp.maximum(1.0 - alphas, KEEP_MIN))
        log_high, log_low = two_parts(log_keep)
        before = before_ref[...]
        after = after_ref[...]
        ahead = nn_dot(log_high, before) + nn_dot(log_low, before)
        weights = jnp.exp(ahead) * alphas
        w_high, w_low = two_parts(weights)

        col_parts = [two_parts(c) for c in colours]
        col_high = [p[0].astype(F32) for p in col_parts]
        col_low = [p[1].astype(F32) for p in col_parts]
        empty = [jnp.zeros((1, entries), F32)]
        col_stack = jnp.concatenate(col_high + col_low + empty * 10, axis=0).astype(BF)
        first = nt_dot(col_stack, w_high)
        second = nt_dot(col_stack, w_low)
        painted = [first[c : c + 1] + (first[3 + c : 4 + c] + second[c : c + 1]) for c in range(3)]
        residual = []
        for c in range(3):
            image_ref[c, pl.ds(tile, 1), :] = painted[c]
            residual.append(painted[c] - goal_ref[c, pl.ds(tile, 1), :])
        res_parts = [two_parts(c) for c in residual]
        res_high = [p[0].astype(F32) for p in res_parts]
        res_low = [p[1].astype(F32) for p in res_parts]
        blank = [jnp.zeros((1, pixels), F32)]
        res_left = jnp.concatenate(res_high + res_high + res_low + blank * 7, axis=0).astype(BF)
        col_right = jnp.concatenate(col_high + col_low + col_high + empty * 7, axis=0).astype(BF)
        weight_pull = tn_dot(res_left, col_right)
        res_stack = jnp.concatenate(res_high + res_low + blank * 10, axis=0).astype(BF)
        pull_one = nn_dot(res_stack, w_high)
        pull_two = nn_dot(res_stack, w_low)
        col_grads = [
            pull_one[c : c + 1] + (pull_one[3 + c : 4 + c] + pull_two[c : c + 1]) for c in range(3)
        ]
        share = weight_pull * weights
        s_high, s_low = two_parts(share)
        behind = nn_dot(s_high, after) + nn_dot(s_low, after)
        odds = jnp.exp2(power - log_keep * LOG2E)
        pull = share - odds * behind

        sum0 = jnp.zeros((TILE_PX, entries), F32)
        sum1 = sum0
        sum2 = sum0
        for y in range(TILE_PX - 1, -1, -1):
            sum0 = sum0 + pull[y * TILE_PX : (y + 1) * TILE_PX]
            sum1 = sum1 + sum0
            sum2 = sum2 + sum1
        first_y = sum1 - 8.5 * sum0
        second_y = 2.0 * sum2 - 18.0 * sum1 + 72.25 * sum0

        def over_x(value):
            return jnp.sum(value, axis=0, keepdims=True)

        m00 = over_x(sum0)
        m10 = over_x(spot * sum0)
        m20 = over_x(spot * spot * sum0)
        m01 = over_x(first_y)
        m11 = over_x(spot * first_y)
        m02 = over_x(second_y)
        by_x = m10 - rec_u * m00
        by_y = m01 - rec_v * m00
        by_xx = m20 - rec_u * (2.0 * m10 - rec_u * m00)
        by_xy = m11 - rec_u * m01 - rec_v * (m10 - rec_u * m00)
        by_yy = m02 - rec_v * (2.0 * m01 - rec_v * m00)
        grads = [
            con_a * by_x + con_b * by_y,
            con_c * by_y + con_b * by_x,
            -0.5 * by_xx,
            -by_xy,
            -0.5 * by_yy,
            col_grads[0],
            col_grads[1],
            col_grads[2],
            m00,
        ]
        total_ref[...] += put_into(grads, index)

    def body(step, carry):
        tile_step(step)
        return carry

    lax.fori_loop(0, tiles, body, 0)
    for h in range(2):
        for r in range(9):
            for i in range(0, HALF, 8):
                grads_ref[pl.ds((h * HALF + i) * 16 + r, 8, stride=16), :] = total_ref[
                    r * HALF + i : r * HALF + i + 8, h * LANES : (h + 1) * LANES
                ]


def render(counts, ids, got, lists, goal):
    tiles, entries = lists.shape
    vmem = pl.BlockSpec(memory_space=pltpu.VMEM)
    smem = pl.BlockSpec(memory_space=pltpu.SMEM)
    return pl.pallas_call(
        render_kernel,
        in_specs=[smem, smem, vmem, vmem, vmem],
        out_specs=[vmem, vmem],
        out_shape=[
            jax.ShapeDtypeStruct(goal.shape, F32),
            jax.ShapeDtypeStruct(got.shape, F32),
        ],
        scratch_shapes=[
            pltpu.VMEM((9 * HALF, 2 * WIDE), BF),
            pltpu.VMEM((2 * HALF, WIDE), BF),
            pltpu.VMEM((entries, entries), BF),
            pltpu.VMEM((entries, entries), BF),
            pltpu.VMEM((9 * HALF, WIDE), F32),
        ],
        compiler_params=pltpu.CompilerParams(vmem_limit_bytes=48 << 20),
        name="render",
    )(counts, ids, got, lists, goal)


def collect_kernel(wanted_ref, back_ref, out_ref, total_ref):
    steps = wanted_ref.shape[0] // 2
    per_cam = steps // 4
    total_ref[...] = jnp.zeros_like(total_ref)

    def body(step, carry):
        index = pair_of(wanted_ref, step)
        left = back_ref[2 * step, 0:9, :]
        right = back_ref[2 * step + 1, 0:9, :]
        block = jnp.concatenate([left, right], axis=1)
        viewer = jnp.full((1, WIDE), step // per_cam, jnp.int32).astype(F32)
        rows = [block[r : r + 1] for r in range(9)] + [viewer]
        total_ref[...] += put_into(rows, index)
        return carry

    lax.fori_loop(0, steps, body, 0, unroll=2)
    for r in range(10):
        for h in range(2):
            out_ref[r, h * HALF : (h + 1) * HALF, :] = total_ref[
                r * HALF : (r + 1) * HALF, h * LANES : (h + 1) * LANES
            ]


def collect(wanted, back):
    return pl.pallas_call(
        collect_kernel,
        in_specs=[pl.BlockSpec(memory_space=pltpu.VMEM)] * 2,
        out_specs=pl.BlockSpec(memory_space=pltpu.VMEM),
        out_shape=jax.ShapeDtypeStruct((10, 2 * HALF, LANES), F32),
        scratch_shapes=[pltpu.VMEM((10 * HALF, WIDE), F32)],
        compiler_params=pltpu.CompilerParams(vmem_limit_bytes=48 << 20),
        name="collect",
    )(wanted, back)


def step_size(row):
    if row < 3:
        return 0.00016
    if row < 6:
        return 0.005
    if row < 10:
        return 0.001
    if row < 11:
        return 0.025
    if row < 14:
        return 0.0025
    return 0.000125


def adam_kernel(turn_ref, shift_ref, pulls_ref, params_ref, one_ref, two_ref, new_ref, new_one_ref, new_two_ref):
    columns = params_ref.shape[1]
    total = params_ref.shape[0]
    rows = columns // LANES
    params = dense_rows(params_ref, columns)
    viewer = pulls_ref[9]
    matrix, eye = camera_of(turn_ref, shift_ref, 0, (rows, LANES))
    for cam in range(1, 4):
        here = viewer > cam - 0.5
        other, other_eye = camera_of(turn_ref, shift_ref, cam, (rows, LANES))
        matrix = [[jnp.where(here, other[i][j], matrix[i][j]) for j in range(3)] for i in range(3)]
        eye = [jnp.where(here, other_eye[i], eye[i]) for i in range(3)]
    _, pull_back = jax.vjp(lambda *values: project(values, matrix, eye), *params)
    grads = list(pull_back([pulls_ref[r] for r in range(8)]))
    grads[10] = pulls_ref[8] * jax.nn.sigmoid(-params[10])
    for start in range(0, total, 8):
        size = min(8, total - start)
        gradient = jnp.stack(grads[start : start + size], axis=0).reshape(size, columns)
        at = pl.ds(start, size)
        new_one = BETA_ONE * one_ref[at, :] + (1.0 - BETA_ONE) * gradient
        new_two = BETA_TWO * two_ref[at, :] + (1.0 - BETA_TWO) * gradient * gradient
        sizes = [step_size(row) / BIAS_ONE for row in range(start, start + size)]
        rate = jnp.full((size, 1), sizes[0], F32)
        which = lax.broadcasted_iota(jnp.int32, (size, 1), 0)
        for k in range(1, size):
            if sizes[k] != sizes[k - 1]:
                rate = jnp.where(which >= k, sizes[k], rate)
        new_one_ref[at, :] = new_one
        new_two_ref[at, :] = new_two
        new_ref[at, :] = params_ref[at, :] - rate * new_one / (
            jnp.sqrt(new_two * (1.0 / BIAS_TWO)) + ADAM_EPS
        )


def apply_adam(pulls, params, one, two, camera_turn, camera_shift):
    rows_in, own_count = params.shape
    columns = 1024
    block = pl.BlockSpec((rows_in, columns), lambda i: (0, i))
    return pl.pallas_call(
        adam_kernel,
        grid=(own_count // columns,),
        in_specs=[
            pl.BlockSpec(memory_space=pltpu.SMEM),
            pl.BlockSpec(memory_space=pltpu.SMEM),
            pl.BlockSpec((10, columns // LANES, LANES), lambda i: (0, i, 0)),
            block,
            block,
            block,
        ],
        out_specs=[block] * 3,
        out_shape=[jax.ShapeDtypeStruct(params.shape, F32)] * 3,
        compiler_params=pltpu.CompilerParams(vmem_limit_bytes=48 << 20),
        name="apply_adam",
    )(camera_turn, camera_shift, pulls, params, one, two)


def exchange(outgoing):
    return lax.all_to_all(outgoing, ("cam", "tile"), split_axis=0, concat_axis=0, tiled=True)


def shards(
    splat_params,
    first_moment,
    second_moment,
    camera_turn,
    camera_shift,
    fetch_table,
    tile_lists,
    tile_counts,
    tile_ids,
    target_image,
):
    devices, capacity = fetch_table.shape[1:]
    wanted = exchange(fetch_table[0])
    table, low = project_all(splat_params, camera_turn, camera_shift)
    arrived = exchange(answer(wanted, table, low))
    rendered, slot_grads = render(
        tile_counts, tile_ids, arrived.reshape(devices * 16, capacity), tile_lists[0], target_image[:, 0]
    )
    returned = exchange(slot_grads.reshape(devices, 16, capacity))
    pulls = collect(wanted, returned)
    updated_params, updated_first, updated_second = apply_adam(
        pulls, splat_params, first_moment, second_moment, camera_turn, camera_shift
    )
    return (updated_params, updated_first, updated_second, rendered[:, None])


def solution(mesh):
    return jax.shard_map(
        shards,
        mesh=mesh,
        in_specs=(
            P(None, ("cam", "tile")),
            P(None, ("cam", "tile")),
            P(None, ("cam", "tile")),
            P(),
            P(),
            P(("cam", "tile"), None, None),
            P("cam", "tile", None),
            P("cam", "tile"),
            P("cam", "tile"),
            P(None, "cam", "tile", None),
        ),
        out_specs=(
            P(None, ("cam", "tile")),
            P(None, ("cam", "tile")),
            P(None, ("cam", "tile")),
            P(None, "cam", "tile", None),
        ),
        check_vma=False,
    )
```

```python
import functools
import math

import jax
import jax.numpy as jnp
from jax import lax
from jax.experimental import pallas as pl
from jax.experimental.pallas import tpu as pltpu
from jax.sharding import PartitionSpec as P

TILE_PX = 16
GRID = 32


FOCAL = 512.0
CENTRE = 256.0
EYE_GAP = 20.0
DILATION = 0.3
SH_ZERO = 0.28209479177387814
SH_ONE = 0.4886025119029199
SH_TWO = (
    1.0925484305920792,
    -1.0925484305920792,
    0.31539156525252005,
    -1.0925484305920792,
    0.5462742152960396,
)
SH_THREE = (
    -0.5900435899266435,
    2.890611442640554,
    -0.4570457994644658,
    0.3731763325901154,
    -0.4570457994644658,
    1.445305721320277,
    -0.5900435899266435,
)
BETA_ONE = 0.9
BETA_TWO = 0.999
BIAS_ONE = 1.0 - math.exp(2000.0 * math.log(0.9))
BIAS_TWO = 1.0 - math.exp(2000.0 * math.log(0.999))
ADAM_EPS = 1e-08


def harmonics(dir_x, dir_y, dir_z):
    sq_x = dir_x * dir_x
    sq_y = dir_y * dir_y
    sq_z = dir_z * dir_z
    return [
        SH_ZERO * jnp.ones_like(dir_x),
        -SH_ONE * dir_y,
        SH_ONE * dir_z,
        -SH_ONE * dir_x,
        SH_TWO[0] * dir_x * dir_y,
        SH_TWO[1] * dir_y * dir_z,
        SH_TWO[2] * (2.0 * sq_z - sq_x - sq_y),
        SH_TWO[3] * dir_x * dir_z,
        SH_TWO[4] * (sq_x - sq_y),
        SH_THREE[0] * dir_y * (3.0 * sq_x - sq_y),
        SH_THREE[1] * dir_x * dir_y * dir_z,
        SH_THREE[2] * dir_y * (4.0 * sq_z - sq_x - sq_y),
        SH_THREE[3] * dir_z * (2.0 * sq_z - 3.0 * sq_x - 3.0 * sq_y),
        SH_THREE[4] * dir_x * (4.0 * sq_z - sq_x - sq_y),
        SH_THREE[5] * dir_z * (sq_x - sq_y),
        SH_THREE[6] * dir_x * (sq_x - 3.0 * sq_y),
    ]


def quat_matrix(quat_w, quat_x, quat_y, quat_z):
    return [
        [
            1.0 - 2.0 * (quat_y * quat_y + quat_z * quat_z),
            2.0 * (quat_x * quat_y - quat_w * quat_z),
            2.0 * (quat_x * quat_z + quat_w * quat_y),
        ],
        [
            2.0 * (quat_x * quat_y + quat_w * quat_z),
            1.0 - 2.0 * (quat_x * quat_x + quat_z * quat_z),
            2.0 * (quat_y * quat_z - quat_w * quat_x),
        ],
        [
            2.0 * (quat_x * quat_z - quat_w * quat_y),
            2.0 * (quat_y * quat_z + quat_w * quat_x),
            1.0 - 2.0 * (quat_x * quat_x + quat_y * quat_y),
        ],
    ]

LOG2E = math.log2(math.e)
HALF = 64
WIDE = 256
LANES = 128
BIG = 3e38
DEAD = -1e4
KEEP_MIN = 2.0**-24
BF = jnp.bfloat16
F32 = jnp.float32


def project(params, camera, eye_pos):
    scales = [jnp.exp(params[3 + i]) for i in range(3)]
    norm_quat = jnp.sqrt(
        params[6] * params[6]
        + params[7] * params[7]
        + params[8] * params[8]
        + params[9] * params[9]
    )
    rotation = quat_matrix(
        params[6] / norm_quat, params[7] / norm_quat, params[8] / norm_quat, params[9] / norm_quat
    )
    relative = [params[i] - eye_pos[i] for i in range(3)]
    in_view = [
        camera[i][0] * relative[0] + camera[i][1] * relative[1] + camera[i][2] * relative[2]
        for i in range(3)
    ]
    inv_depth = 1.0 / in_view[2]
    screen_x = FOCAL * in_view[0] * inv_depth + CENTRE
    screen_y = FOCAL * in_view[1] * inv_depth + CENTRE
    axes_cam = [
        [
            (
                camera[i][0] * rotation[0][k]
                + camera[i][1] * rotation[1][k]
                + camera[i][2] * rotation[2][k]
            )
            * scales[k]
            for k in range(3)
        ]
        for i in range(3)
    ]
    slope_x = FOCAL * in_view[0] * inv_depth * inv_depth
    slope_y = FOCAL * in_view[1] * inv_depth * inv_depth
    row_x = [FOCAL * inv_depth * axes_cam[0][k] - slope_x * axes_cam[2][k] for k in range(3)]
    row_y = [FOCAL * inv_depth * axes_cam[1][k] - slope_y * axes_cam[2][k] for k in range(3)]
    cov_xx = row_x[0] * row_x[0] + row_x[1] * row_x[1] + row_x[2] * row_x[2] + DILATION
    cov_xy = row_x[0] * row_y[0] + row_x[1] * row_y[1] + row_x[2] * row_y[2]
    cov_yy = row_y[0] * row_y[0] + row_y[1] * row_y[1] + row_y[2] * row_y[2] + DILATION
    inv_det = 1.0 / (cov_xx * cov_yy - cov_xy * cov_xy)
    inv_dist = 1.0 / jnp.sqrt(
        relative[0] * relative[0] + relative[1] * relative[1] + relative[2] * relative[2]
    )
    basis = harmonics(relative[0] * inv_dist, relative[1] * inv_dist, relative[2] * inv_dist)
    colours = []
    for channel in range(3):
        total = basis[0] * params[11 + channel]
        for k in range(1, 16):
            total = total + basis[k] * params[11 + 3 * k + channel]
        colours.append(jnp.maximum(total + 0.5, 0.0))
    return [
        screen_x,
        screen_y,
        cov_yy * inv_det,
        -cov_xy * inv_det,
        cov_xx * inv_det,
        colours[0],
        colours[1],
        colours[2],
    ]


def camera_of(turn_ref, shift_ref, cam, shape):
    turn = [jnp.full(shape, turn_ref[cam, i], F32) for i in range(3)]
    norm = jnp.sqrt(1.0 + (turn[0] * turn[0] + turn[1] * turn[1] + turn[2] * turn[2]))
    matrix = quat_matrix(1.0 / norm, turn[0] / norm, turn[1] / norm, turn[2] / norm)
    eye = [jnp.full(shape, shift_ref[cam, i], F32) for i in range(3)]
    eye[0] = EYE_GAP * cam + eye[0]
    return matrix, eye


def dense_rows(ref, columns):
    rows = []
    total = ref.shape[0]
    for start in range(0, total, 8):
        size = min(8, total - start)
        block = ref[start : start + size, :].reshape(size, columns // LANES, LANES)
        rows.extend(block[r] for r in range(size))
    return rows


def two_parts(value):
    high = value.astype(BF)
    return high, (value - high.astype(F32)).astype(BF)


def nt_dot(lhs, rhs):
    return lax.dot_general(lhs, rhs, (((1,), (1,)), ((), ())), preferred_element_type=F32)


def tn_dot(lhs, rhs):
    return lax.dot_general(lhs, rhs, (((0,), (0,)), ((), ())), preferred_element_type=F32)


def nn_dot(lhs, rhs):
    return lax.dot_general(lhs, rhs, (((1,), (0,)), ((), ())), preferred_element_type=F32)


def one_hots(index):
    count = index.shape[1]
    wide = ((index >> 13) * LANES + (index & 127)).astype(F32).astype(BF)
    narrow = ((index >> 7) & 63).astype(F32)
    one = jnp.ones((), BF)
    zero = jnp.zeros((), BF)
    rows = lax.broadcasted_iota(jnp.int32, (WIDE, count), 0).astype(F32).astype(BF)
    pick = jnp.where(rows == wide, one, zero)
    few = lax.broadcasted_iota(jnp.int32, (HALF, count), 0).astype(F32)
    return pick, jnp.where(few == narrow, 1.0, 0.0)


def pick_from(table, low_table, index):
    pick, mask = one_hots(index)
    spread = nn_dot(table, jnp.concatenate([pick, pick], axis=0))
    extra = nn_dot(low_table, pick)
    picked = []
    for r in range(9):
        part = spread[r * HALF : (r + 1) * HALF]
        if r < 2:
            part = part + extra[r * HALF : (r + 1) * HALF]
        picked.append(jnp.sum(part * mask, axis=0, keepdims=True))
    return picked


def put_into(rows, index):
    pick, mask = one_hots(index)
    mask = mask.astype(BF)
    parts = [two_parts(row) for row in rows]
    high = jnp.concatenate([mask * part[0] for part in parts], axis=0)
    low = jnp.concatenate([mask * part[1] for part in parts], axis=0)
    return nt_dot(jnp.concatenate([high, low], axis=1), jnp.concatenate([pick, pick], axis=1))


MESH = pl.DeviceIdType.MESH


def signal_all(barrier, cams, tiles):
    own_cam = lax.axis_index("cam")
    own_tile = lax.axis_index("tile")
    for step in range(cams):
        cam = lax.rem(own_cam + step, cams)

        def tell(i, carry, cam=cam):
            pl.semaphore_signal(
                barrier, inc=1, device_id=(cam, lax.rem(own_tile + i, tiles)), device_id_type=MESH
            )
            return carry

        lax.fori_loop(1 if step == 0 else 0, tiles, tell, 0, unroll=4)


def project_block(turn_ref, shift_ref, params_ref, table_ref, low_ref, half, step, columns):
    rows = columns // LANES
    start = pl.multiple_of(half * (HALF * LANES) + step * columns, columns)
    params = []
    total = params_ref.shape[0]
    for first in range(0, total, 8):
        size = min(8, total - first)
        block = params_ref[first : first + size, pl.ds(start, columns)].reshape(size, rows, LANES)
        params.extend(block[r] for r in range(size))
    opacity = jax.nn.sigmoid(params[10])
    at = half * LANES
    place = pl.ds(pl.multiple_of(step * rows, rows), rows)
    for cam in range(4):
        matrix, eye = camera_of(turn_ref, shift_ref, cam, (rows, LANES))
        record = project(params, matrix, eye) + [opacity]
        for r, value in enumerate(record):
            value = jnp.where(value == value, jnp.clip(value, -BIG, BIG), 0.0)
            high, mid = two_parts(value)
            table_ref[cam, r, place, at : at + LANES] = high
            table_ref[cam, r, place, WIDE + at : WIDE + at + LANES] = mid
            if r < 2:
                low = (value - high.astype(F32)) - mid.astype(F32)
                low_ref[cam, r, place, at : at + LANES] = low.astype(BF)


def ask_kernel(
    cams, tiles, turn_ref, shift_ref, fetch_ref, params_ref, wanted_ref, table_ref, low_ref,
    held_ref, send_sem, recv_sem, own_sem, load_sem,
):
    columns = 2048
    steps = HALF * LANES // columns
    load = pltpu.make_async_copy(params_ref, held_ref, load_sem)
    load.start()
    barrier = pltpu.get_barrier_semaphore()
    signal_all(barrier, cams, tiles)
    own_cam = lax.axis_index("cam")
    own_tile = lax.axis_index("tile")
    me = own_cam * tiles + own_tile
    others = cams * tiles - 1
    own = pltpu.make_async_copy(fetch_ref.at[me], wanted_ref.at[me], own_sem)
    own.start()
    pl.semaphore_wait(barrier, others)
    for hop in range(cams):
        cam = lax.rem(own_cam + hop, cams)

        def ask(i, carry, cam=cam):
            tile = lax.rem(own_tile + i, tiles)
            pltpu.make_async_remote_copy(
                src_ref=fetch_ref.at[cam * tiles + tile],
                dst_ref=wanted_ref.at[me],
                send_sem=send_sem,
                recv_sem=recv_sem,
                device_id=(cam, tile),
                device_id_type=MESH,
            ).start()
            return carry

        lax.fori_loop(1 if hop == 0 else 0, tiles, ask, 0, unroll=4)
    load.wait()

    def body(step, carry):
        for half in range(2):
            project_block(turn_ref, shift_ref, held_ref, table_ref, low_ref, half, step, columns)
        return carry

    lax.fori_loop(0, steps, body, 0)
    own.wait()
    many = pl.ds(0, others)
    pltpu.make_async_copy(fetch_ref.at[many], wanted_ref.at[many], send_sem).wait()
    pltpu.make_async_copy(fetch_ref.at[many], wanted_ref.at[many], recv_sem).wait()


def ask_and_project(mesh_shape, fetch, splat_params, camera_turn, camera_shift):
    vmem = pl.BlockSpec(memory_space=pltpu.VMEM)
    smem = pl.BlockSpec(memory_space=pltpu.SMEM)
    return pl.pallas_call(
        functools.partial(ask_kernel, *mesh_shape),
        in_specs=[smem, smem, vmem, pl.BlockSpec(memory_space=pl.ANY)],
        out_specs=[vmem] * 3,
        out_shape=[
            jax.ShapeDtypeStruct(fetch.shape, jnp.int32),
            jax.ShapeDtypeStruct((4, 9, HALF, 2 * WIDE), BF),
            jax.ShapeDtypeStruct((4, 2, HALF, WIDE), BF),
        ],
        scratch_shapes=[pltpu.VMEM(splat_params.shape, F32)] + [pltpu.SemaphoreType.DMA(())] * 4,
        compiler_params=pltpu.CompilerParams(
            vmem_limit_bytes=48 << 20, collective_id=0, has_side_effects=True
        ),
        name="ask_and_project",
    )(camera_turn, camera_shift, fetch, splat_params)


def pair_of(ref, chip):
    return jnp.concatenate([ref[2 * chip], ref[2 * chip + 1]], axis=1)


def answer_kernel(cams, tiles, wanted_ref, table_ref, low_ref, got_ref, held_ref, send_sem, recv_sem, own_sem):
    chips = cams * tiles // 2
    per_cam = chips // cams
    others = 2 * chips - 1
    me = lax.axis_index("cam") * tiles + lax.axis_index("tile")
    own_chip = me // 2
    twin = 2 * own_chip + (1 - lax.rem(me, 2))
    barrier = pltpu.get_barrier_semaphore()
    signal_all(barrier, cams, tiles)

    def fill(chip):
        picked = pick_from(
            table_ref[chip // per_cam].reshape(9 * HALF, 2 * WIDE),
            low_ref[chip // per_cam].reshape(2 * HALF, WIDE),
            pair_of(wanted_ref, chip),
        )
        block = jnp.concatenate(picked, axis=0)
        held_ref[2 * chip, 0:9, :] = block[:, :LANES]
        held_ref[2 * chip + 1, 0:9, :] = block[:, LANES:]

    def send(other):
        pltpu.make_async_remote_copy(
            src_ref=held_ref.at[other, 0:9],
            dst_ref=got_ref.at[me, 0:9],
            send_sem=send_sem,
            recv_sem=recv_sem,
            device_id=(other // tiles, lax.rem(other, tiles)),
            device_id_type=MESH,
        ).start()

    per_batch = 4

    def fill_batch(batch):
        for k in range(per_batch):
            fill(lax.rem(own_chip + batch * per_batch + k, chips))

    def send_chip(step):
        chip = lax.rem(own_chip + step, chips)
        send(2 * chip)
        send(2 * chip + 1)

    fill_batch(0)
    own = pltpu.make_async_copy(held_ref.at[me, 0:9], got_ref.at[me, 0:9], own_sem)
    own.start()
    pl.semaphore_wait(barrier, others)
    send(twin)
    for k in range(1, per_batch):
        send_chip(k)

    def body(batch, carry):
        fill_batch(batch)
        for k in range(per_batch):
            send_chip(batch * per_batch + k)
        return carry

    lax.fori_loop(1, chips // per_batch, body, 0)
    own.wait()
    many = pl.ds(0, others)
    pltpu.make_async_copy(held_ref.at[many, 0:9], got_ref.at[many, 0:9], send_sem).wait()
    pltpu.make_async_copy(held_ref.at[many, 0:9], got_ref.at[many, 0:9], recv_sem).wait()


def answer(mesh_shape, wanted, table, low):
    devices, _, capacity = wanted.shape
    shape = (devices, 16, capacity)
    return pl.pallas_call(
        functools.partial(answer_kernel, *mesh_shape),
        in_specs=[pl.BlockSpec(memory_space=pltpu.VMEM)] * 3,
        out_specs=pl.BlockSpec(memory_space=pltpu.VMEM),
        out_shape=jax.ShapeDtypeStruct(shape, F32),
        scratch_shapes=[pltpu.VMEM(shape, F32)] + [pltpu.SemaphoreType.DMA(())] * 3,
        compiler_params=pltpu.CompilerParams(
            vmem_limit_bytes=48 << 20, collective_id=1, has_side_effects=True
        ),
        name="answer",
    )(wanted, table, low)


def render_kernel(
    counts_ref, ids_ref, got_ref, lists_ref, goal_ref, image_ref, grads_ref,
    table_ref, low_ref, before_ref, after_ref, total_ref,
):
    tiles, entries = lists_ref.shape
    pixels = goal_ref.shape[2]

    for h in range(2):
        for r in range(9):
            value = jnp.concatenate(
                [got_ref[pl.ds((h * HALF + i) * 16 + r, 8, stride=16), :] for i in range(0, HALF, 8)], axis=0
            )
            high, mid = two_parts(value)
            table_ref[r * HALF : (r + 1) * HALF, h * LANES : (h + 1) * LANES] = high
            table_ref[r * HALF : (r + 1) * HALF, WIDE + h * LANES : WIDE + (h + 1) * LANES] = mid
            if r < 2:
                low = (value - high.astype(F32)) - mid.astype(F32)
                low_ref[r * HALF : (r + 1) * HALF, h * LANES : (h + 1) * LANES] = low.astype(BF)
    row = lax.broadcasted_iota(jnp.int32, (entries, entries), 0)
    col = lax.broadcasted_iota(jnp.int32, (entries, entries), 1)
    before_ref[...] = jnp.where(row < col, 1.0, 0.0).astype(BF)
    after_ref[...] = jnp.where(row > col, 1.0, 0.0).astype(BF)
    total_ref[...] = jnp.zeros_like(total_ref)

    def tile_step(tile):
        index = lists_ref[pl.ds(tile, 1), :]
        live = lax.broadcasted_iota(jnp.int32, (1, entries), 1) < counts_ref[0, tile]
        number = ids_ref[0, tile]
        origin_x = ((number & 31) * TILE_PX + TILE_PX // 2).astype(F32)
        origin_y = ((number >> 5) * TILE_PX + TILE_PX // 2).astype(F32)
        rec = pick_from(table_ref[...], low_ref[...], index)
        rec_u = jnp.where(live, rec[0] - origin_x, 0.0)
        rec_v = jnp.where(live, rec[1] - origin_y, 0.0)
        con_a = jnp.where(live, rec[2], 0.0)
        con_b = jnp.where(live, rec[3], 0.0)
        con_c = jnp.where(live, rec[4], 0.0)
        log_o = jnp.where(live, jnp.maximum(jnp.log(rec[8]) * LOG2E, DEAD), DEAD)
        colours = rec[5:8]

        spot = lax.broadcasted_iota(jnp.int32, (TILE_PX, entries), 0).astype(F32) - 7.5
        off_x = spot - rec_u
        off_y = spot - rec_v
        part_x = (-0.5 * LOG2E) * con_a * off_x * off_x + log_o
        cross = (-LOG2E) * con_b * off_x
        part_y = (-0.5 * LOG2E) * con_c * off_y * off_y
        power = jnp.concatenate(
            [part_x + (cross * off_y[y : y + 1] + part_y[y : y + 1]) for y in range(TILE_PX)], axis=0
        )
        alphas = jnp.exp2(power)
        log_keep = jnp.log(jnp.maximum(1.0 - alphas, KEEP_MIN))
        log_high, log_low = two_parts(log_keep)
        before = before_ref[...]
        after = after_ref[...]
        ahead = nn_dot(log_high, before) + nn_dot(log_low, before)
        weights = jnp.exp(ahead) * alphas
        w_high, w_low = two_parts(weights)

        col_parts = [two_parts(c) for c in colours]
        col_high = [p[0].astype(F32) for p in col_parts]
        col_low = [p[1].astype(F32) for p in col_parts]
        empty = [jnp.zeros((1, entries), F32)]
        col_stack = jnp.concatenate(col_high + col_low + empty * 10, axis=0).astype(BF)
        first = nt_dot(col_stack, w_high)
        second = nt_dot(col_stack, w_low)
        painted = [first[c : c + 1] + (first[3 + c : 4 + c] + second[c : c + 1]) for c in range(3)]
        residual = []
        for c in range(3):
            image_ref[c, pl.ds(tile, 1), :] = painted[c]
            residual.append(painted[c] - goal_ref[c, pl.ds(tile, 1), :])
        res_parts = [two_parts(c) for c in residual]
        res_high = [p[0].astype(F32) for p in res_parts]
        res_low = [p[1].astype(F32) for p in res_parts]
        blank = [jnp.zeros((1, pixels), F32)]
        res_left = jnp.concatenate(res_high + res_high + res_low + blank * 7, axis=0).astype(BF)
        col_right = jnp.concatenate(col_high + col_low + col_high + empty * 7, axis=0).astype(BF)
        weight_pull = tn_dot(res_left, col_right)
        res_stack = jnp.concatenate(res_high + res_low + blank * 10, axis=0).astype(BF)
        pull_one = nn_dot(res_stack, w_high)
        pull_two = nn_dot(res_stack, w_low)
        col_grads = [
            pull_one[c : c + 1] + (pull_one[3 + c : 4 + c] + pull_two[c : c + 1]) for c in range(3)
        ]
        share = weight_pull * weights
        s_high, s_low = two_parts(share)
        behind = nn_dot(s_high, after) + nn_dot(s_low, after)
        odds = jnp.exp2(power - log_keep * LOG2E)
        pull = share - odds * behind

        sum0 = jnp.zeros((TILE_PX, entries), F32)
        sum1 = sum0
        sum2 = sum0
        for y in range(TILE_PX - 1, -1, -1):
            sum0 = sum0 + pull[y * TILE_PX : (y + 1) * TILE_PX]
            sum1 = sum1 + sum0
            sum2 = sum2 + sum1
        first_y = sum1 - 8.5 * sum0
        second_y = 2.0 * sum2 - 18.0 * sum1 + 72.25 * sum0

        def over_x(value):
            return jnp.sum(value, axis=0, keepdims=True)

        m00 = over_x(sum0)
        m10 = over_x(spot * sum0)
        m20 = over_x(spot * spot * sum0)
        m01 = over_x(first_y)
        m11 = over_x(spot * first_y)
        m02 = over_x(second_y)
        by_x = m10 - rec_u * m00
        by_y = m01 - rec_v * m00
        by_xx = m20 - rec_u * (2.0 * m10 - rec_u * m00)
        by_xy = m11 - rec_u * m01 - rec_v * (m10 - rec_u * m00)
        by_yy = m02 - rec_v * (2.0 * m01 - rec_v * m00)
        grads = [
            con_a * by_x + con_b * by_y,
            con_c * by_y + con_b * by_x,
            -0.5 * by_xx,
            -by_xy,
            -0.5 * by_yy,
            col_grads[0],
            col_grads[1],
            col_grads[2],
            m00,
        ]
        total_ref[...] += put_into(grads, index)

    def body(step, carry):
        tile_step(step)
        return carry

    lax.fori_loop(0, tiles, body, 0, unroll=2)
    for h in range(2):
        for r in range(9):
            for i in range(0, HALF, 8):
                grads_ref[pl.ds((h * HALF + i) * 16 + r, 8, stride=16), :] = total_ref[
                    r * HALF + i : r * HALF + i + 8, h * LANES : (h + 1) * LANES
                ]


def render(counts, ids, got, lists, goal):
    tiles, entries = lists.shape
    vmem = pl.BlockSpec(memory_space=pltpu.VMEM)
    smem = pl.BlockSpec(memory_space=pltpu.SMEM)
    return pl.pallas_call(
        render_kernel,
        in_specs=[smem, smem, vmem, vmem, vmem],
        out_specs=[vmem, vmem],
        out_shape=[
            jax.ShapeDtypeStruct(goal.shape, F32),
            jax.ShapeDtypeStruct(got.shape, F32),
        ],
        scratch_shapes=[
            pltpu.VMEM((9 * HALF, 2 * WIDE), BF),
            pltpu.VMEM((2 * HALF, WIDE), BF),
            pltpu.VMEM((entries, entries), BF),
            pltpu.VMEM((entries, entries), BF),
            pltpu.VMEM((9 * HALF, WIDE), F32),
        ],
        compiler_params=pltpu.CompilerParams(vmem_limit_bytes=48 << 20),
        name="render",
    )(counts, ids, got, lists, goal)


def collect_kernel(
    cams, tiles, wanted_ref, away_ref, out_ref, back_ref, total_ref, send_sem, recv_sem
):
    chips = cams * tiles // 2
    per_cam = chips // cams
    per_group = 4
    groups = chips // per_group
    others = 2 * chips - 1
    me = lax.axis_index("cam") * tiles + lax.axis_index("tile")
    own_chip = me // 2
    twin = 2 * own_chip + (1 - lax.rem(me, 2))
    barrier = pltpu.get_barrier_semaphore()
    signal_all(barrier, cams, tiles)
    own = pltpu.make_async_copy(away_ref.at[me, 0:9], back_ref.at[me, 0:9], recv_sem.at[0])
    own.start()
    total_ref[...] = jnp.zeros_like(total_ref)
    pl.semaphore_wait(barrier, others)

    def send(other, group):
        pltpu.make_async_remote_copy(
            src_ref=away_ref.at[other, 0:9],
            dst_ref=back_ref.at[me, 0:9],
            send_sem=send_sem,
            recv_sem=recv_sem.at[group],
            device_id=(other // tiles, lax.rem(other, tiles)),
            device_id_type=MESH,
        ).start()

    send(twin, 0)

    def give(step, carry):
        chip = lax.rem(own_chip + step, chips)
        send(2 * chip, step // per_group)
        send(2 * chip + 1, step // per_group)
        return carry

    lax.fori_loop(1, chips, give, 0, unroll=3)

    def take(group, carry):
        block = pl.ds(0, 2 * per_group)
        pltpu.make_async_copy(away_ref.at[block, 0:9], back_ref.at[block, 0:9], recv_sem.at[group]).wait()
        for k in range(per_group):
            chip = lax.rem(own_chip + chips - (group * per_group + k), chips)
            both = jnp.concatenate([back_ref[2 * chip, 0:9, :], back_ref[2 * chip + 1, 0:9, :]], axis=1)
            viewer = jnp.full((1, WIDE), chip // per_cam, jnp.int32).astype(F32)
            rows = [both[r : r + 1] for r in range(9)] + [viewer]
            total_ref[...] += put_into(rows, pair_of(wanted_ref, chip))
        return carry

    lax.fori_loop(0, groups, take, 0)
    for r in range(10):
        for h in range(2):
            out_ref[r, h * HALF : (h + 1) * HALF, :] = total_ref[
                r * HALF : (r + 1) * HALF, h * LANES : (h + 1) * LANES
            ]
    many = pl.ds(0, others)
    pltpu.make_async_copy(away_ref.at[many, 0:9], back_ref.at[many, 0:9], send_sem).wait()


def collect(mesh_shape, wanted, away):
    chips = mesh_shape[0] * mesh_shape[1] // 2
    return pl.pallas_call(
        functools.partial(collect_kernel, *mesh_shape),
        in_specs=[pl.BlockSpec(memory_space=pltpu.VMEM)] * 2,
        out_specs=pl.BlockSpec(memory_space=pltpu.VMEM),
        out_shape=jax.ShapeDtypeStruct((10, 2 * HALF, LANES), F32),
        scratch_shapes=[
            pltpu.VMEM(away.shape, F32),
            pltpu.VMEM((10 * HALF, WIDE), F32),
            pltpu.SemaphoreType.DMA(()),
            pltpu.SemaphoreType.DMA((chips // 4,)),
        ],
        compiler_params=pltpu.CompilerParams(
            vmem_limit_bytes=48 << 20, collective_id=2, has_side_effects=True
        ),
        name="collect",
    )(wanted, away)


def step_size(row):
    if row < 3:
        return 0.00016
    if row < 6:
        return 0.005
    if row < 10:
        return 0.001
    if row < 11:
        return 0.025
    if row < 14:
        return 0.0025
    return 0.000125


def adam_kernel(turn_ref, shift_ref, pulls_ref, params_ref, one_ref, two_ref, new_ref, new_one_ref, new_two_ref):
    columns = params_ref.shape[1]
    total = params_ref.shape[0]
    rows = columns // LANES
    params = dense_rows(params_ref, columns)
    viewer = pulls_ref[9]
    matrix, eye = camera_of(turn_ref, shift_ref, 0, (rows, LANES))
    for cam in range(1, 4):
        here = viewer > cam - 0.5
        other, other_eye = camera_of(turn_ref, shift_ref, cam, (rows, LANES))
        matrix = [[jnp.where(here, other[i][j], matrix[i][j]) for j in range(3)] for i in range(3)]
        eye = [jnp.where(here, other_eye[i], eye[i]) for i in range(3)]
    _, pull_back = jax.vjp(lambda *values: project(values, matrix, eye), *params)
    grads = list(pull_back([pulls_ref[r] for r in range(8)]))
    grads[10] = pulls_ref[8] * jax.nn.sigmoid(-params[10])
    for start in range(0, total, 8):
        size = min(8, total - start)
        gradient = jnp.stack(grads[start : start + size], axis=0).reshape(size, columns)
        at = pl.ds(start, size)
        new_one = BETA_ONE * one_ref[at, :] + (1.0 - BETA_ONE) * gradient
        new_two = BETA_TWO * two_ref[at, :] + (1.0 - BETA_TWO) * gradient * gradient
        sizes = [step_size(row) / BIAS_ONE for row in range(start, start + size)]
        rate = jnp.full((size, 1), sizes[0], F32)
        which = lax.broadcasted_iota(jnp.int32, (size, 1), 0)
        for k in range(1, size):
            if sizes[k] != sizes[k - 1]:
                rate = jnp.where(which >= k, sizes[k], rate)
        new_one_ref[at, :] = new_one
        new_two_ref[at, :] = new_two
        new_ref[at, :] = params_ref[at, :] - rate * new_one / (
            jnp.sqrt(new_two * (1.0 / BIAS_TWO)) + ADAM_EPS
        )


def apply_adam(pulls, params, one, two, camera_turn, camera_shift):
    rows_in, own_count = params.shape
    columns = 1024
    block = pl.BlockSpec((rows_in, columns), lambda i: (0, i))
    return pl.pallas_call(
        adam_kernel,
        grid=(own_count // columns,),
        in_specs=[
            pl.BlockSpec(memory_space=pltpu.SMEM),
            pl.BlockSpec(memory_space=pltpu.SMEM),
            pl.BlockSpec((10, columns // LANES, LANES), lambda i: (0, i, 0)),
            block,
            block,
            block,
        ],
        out_specs=[block] * 3,
        out_shape=[jax.ShapeDtypeStruct(params.shape, F32)] * 3,
        compiler_params=pltpu.CompilerParams(vmem_limit_bytes=48 << 20),
        name="apply_adam",
    )(camera_turn, camera_shift, pulls, params, one, two)


def shards(
    splat_params,
    first_moment,
    second_moment,
    camera_turn,
    camera_shift,
    fetch_table,
    tile_lists,
    tile_counts,
    tile_ids,
    target_image,
):
    devices, capacity = fetch_table.shape[1:]
    mesh_shape = (lax.axis_size("cam"), lax.axis_size("tile"))
    wanted, table, low = ask_and_project(
        mesh_shape, fetch_table.reshape(devices, 1, capacity), splat_params, camera_turn, camera_shift
    )
    arrived = answer(mesh_shape, wanted, table, low)
    rendered, slot_grads = render(
        tile_counts, tile_ids, arrived.reshape(devices * 16, capacity), tile_lists[0], target_image[:, 0]
    )
    pulls = collect(mesh_shape, wanted, slot_grads.reshape(devices, 16, capacity))
    updated_params, updated_first, updated_second = apply_adam(
        pulls, splat_params, first_moment, second_moment, camera_turn, camera_shift
    )
    return (updated_params, updated_first, updated_second, rendered[:, None])


def solution(mesh):
    return jax.shard_map(
        shards,
        mesh=mesh,
        in_specs=(
            P(None, ("cam", "tile")),
            P(None, ("cam", "tile")),
            P(None, ("cam", "tile")),
            P(),
            P(),
            P(("cam", "tile"), None, None),
            P("cam", "tile", None),
            P("cam", "tile"),
            P("cam", "tile"),
            P(None, "cam", "tile", None),
        ),
        out_specs=(
            P(None, ("cam", "tile")),
            P(None, ("cam", "tile")),
            P(None, ("cam", "tile")),
            P(None, "cam", "tile", None),
        ),
        check_vma=False,
    )
```

```python
import functools
import math

import jax
import jax.numpy as jnp
from jax import lax
from jax.experimental import pallas as pl
from jax.experimental.pallas import tpu as pltpu
from jax.sharding import PartitionSpec as P

TILE_PX = 16
GRID = 32


FOCAL = 512.0
CENTRE = 256.0
EYE_GAP = 20.0
DILATION = 0.3
SH_ZERO = 0.28209479177387814
SH_ONE = 0.4886025119029199
SH_TWO = (
    1.0925484305920792,
    -1.0925484305920792,
    0.31539156525252005,
    -1.0925484305920792,
    0.5462742152960396,
)
SH_THREE = (
    -0.5900435899266435,
    2.890611442640554,
    -0.4570457994644658,
    0.3731763325901154,
    -0.4570457994644658,
    1.445305721320277,
    -0.5900435899266435,
)
BETA_ONE = 0.9
BETA_TWO = 0.999
BIAS_ONE = 1.0 - math.exp(2000.0 * math.log(0.9))
BIAS_TWO = 1.0 - math.exp(2000.0 * math.log(0.999))
ADAM_EPS = 1e-08


def harmonics(dir_x, dir_y, dir_z):
    sq_x = dir_x * dir_x
    sq_y = dir_y * dir_y
    sq_z = dir_z * dir_z
    return [
        SH_ZERO * jnp.ones_like(dir_x),
        -SH_ONE * dir_y,
        SH_ONE * dir_z,
        -SH_ONE * dir_x,
        SH_TWO[0] * dir_x * dir_y,
        SH_TWO[1] * dir_y * dir_z,
        SH_TWO[2] * (2.0 * sq_z - sq_x - sq_y),
        SH_TWO[3] * dir_x * dir_z,
        SH_TWO[4] * (sq_x - sq_y),
        SH_THREE[0] * dir_y * (3.0 * sq_x - sq_y),
        SH_THREE[1] * dir_x * dir_y * dir_z,
        SH_THREE[2] * dir_y * (4.0 * sq_z - sq_x - sq_y),
        SH_THREE[3] * dir_z * (2.0 * sq_z - 3.0 * sq_x - 3.0 * sq_y),
        SH_THREE[4] * dir_x * (4.0 * sq_z - sq_x - sq_y),
        SH_THREE[5] * dir_z * (sq_x - sq_y),
        SH_THREE[6] * dir_x * (sq_x - 3.0 * sq_y),
    ]


def quat_matrix(quat_w, quat_x, quat_y, quat_z):
    return [
        [
            1.0 - 2.0 * (quat_y * quat_y + quat_z * quat_z),
            2.0 * (quat_x * quat_y - quat_w * quat_z),
            2.0 * (quat_x * quat_z + quat_w * quat_y),
        ],
        [
            2.0 * (quat_x * quat_y + quat_w * quat_z),
            1.0 - 2.0 * (quat_x * quat_x + quat_z * quat_z),
            2.0 * (quat_y * quat_z - quat_w * quat_x),
        ],
        [
            2.0 * (quat_x * quat_z - quat_w * quat_y),
            2.0 * (quat_y * quat_z + quat_w * quat_x),
            1.0 - 2.0 * (quat_x * quat_x + quat_y * quat_y),
        ],
    ]

LOG2E = math.log2(math.e)
HALF = 64
WIDE = 256
LANES = 128
BIG = 3e38
BY_LANES = (0, 1, 8)
BY_MATRIX = (2, 3, 4, 5, 6, 7)
DEAD = -1e4
KEEP_MIN = 2.0**-24
BF = jnp.bfloat16
F32 = jnp.float32


def project(params, camera, eye_pos):
    scales = [jnp.exp(params[3 + i]) for i in range(3)]
    norm_quat = jnp.sqrt(
        params[6] * params[6]
        + params[7] * params[7]
        + params[8] * params[8]
        + params[9] * params[9]
    )
    rotation = quat_matrix(
        params[6] / norm_quat, params[7] / norm_quat, params[8] / norm_quat, params[9] / norm_quat
    )
    relative = [params[i] - eye_pos[i] for i in range(3)]
    in_view = [
        camera[i][0] * relative[0] + camera[i][1] * relative[1] + camera[i][2] * relative[2]
        for i in range(3)
    ]
    inv_depth = 1.0 / in_view[2]
    screen_x = FOCAL * in_view[0] * inv_depth + CENTRE
    screen_y = FOCAL * in_view[1] * inv_depth + CENTRE
    axes_cam = [
        [
            (
                camera[i][0] * rotation[0][k]
                + camera[i][1] * rotation[1][k]
                + camera[i][2] * rotation[2][k]
            )
            * scales[k]
            for k in range(3)
        ]
        for i in range(3)
    ]
    slope_x = FOCAL * in_view[0] * inv_depth * inv_depth
    slope_y = FOCAL * in_view[1] * inv_depth * inv_depth
    row_x = [FOCAL * inv_depth * axes_cam[0][k] - slope_x * axes_cam[2][k] for k in range(3)]
    row_y = [FOCAL * inv_depth * axes_cam[1][k] - slope_y * axes_cam[2][k] for k in range(3)]
    cov_xx = row_x[0] * row_x[0] + row_x[1] * row_x[1] + row_x[2] * row_x[2] + DILATION
    cov_xy = row_x[0] * row_y[0] + row_x[1] * row_y[1] + row_x[2] * row_y[2]
    cov_yy = row_y[0] * row_y[0] + row_y[1] * row_y[1] + row_y[2] * row_y[2] + DILATION
    inv_det = 1.0 / (cov_xx * cov_yy - cov_xy * cov_xy)
    inv_dist = 1.0 / jnp.sqrt(
        relative[0] * relative[0] + relative[1] * relative[1] + relative[2] * relative[2]
    )
    basis = harmonics(relative[0] * inv_dist, relative[1] * inv_dist, relative[2] * inv_dist)
    colours = []
    for channel in range(3):
        total = basis[0] * params[11 + channel]
        for k in range(1, 16):
            total = total + basis[k] * params[11 + 3 * k + channel]
        colours.append(jnp.maximum(total + 0.5, 0.0))
    return [
        screen_x,
        screen_y,
        cov_yy * inv_det,
        -cov_xy * inv_det,
        cov_xx * inv_det,
        colours[0],
        colours[1],
        colours[2],
    ]


def camera_of(turn_ref, shift_ref, cam, shape):
    turn = [jnp.full(shape, turn_ref[cam, i], F32) for i in range(3)]
    norm = jnp.sqrt(1.0 + (turn[0] * turn[0] + turn[1] * turn[1] + turn[2] * turn[2]))
    matrix = quat_matrix(1.0 / norm, turn[0] / norm, turn[1] / norm, turn[2] / norm)
    eye = [jnp.full(shape, shift_ref[cam, i], F32) for i in range(3)]
    eye[0] = EYE_GAP * cam + eye[0]
    return matrix, eye


def dense_rows(ref, columns):
    rows = []
    total = ref.shape[0]
    for start in range(0, total, 8):
        size = min(8, total - start)
        block = ref[start : start + size, :].reshape(size, columns // LANES, LANES)
        rows.extend(block[r] for r in range(size))
    return rows


def two_parts(value):
    high = value.astype(BF)
    return high, (value - high.astype(F32)).astype(BF)


def nt_dot(lhs, rhs):
    return lax.dot_general(lhs, rhs, (((1,), (1,)), ((), ())), preferred_element_type=F32)


def tn_dot(lhs, rhs):
    return lax.dot_general(lhs, rhs, (((0,), (0,)), ((), ())), preferred_element_type=F32)


def nn_dot(lhs, rhs):
    return lax.dot_general(lhs, rhs, (((1,), (0,)), ((), ())), preferred_element_type=F32)


def one_hots(index):
    count = index.shape[1]
    wide = ((index >> 13) * LANES + (index & 127)).astype(F32).astype(BF)
    narrow = ((index >> 7) & 63).astype(F32)
    one = jnp.ones((), BF)
    zero = jnp.zeros((), BF)
    rows = lax.broadcasted_iota(jnp.int32, (WIDE, count), 0).astype(F32).astype(BF)
    pick = jnp.where(rows == wide, one, zero)
    few = lax.broadcasted_iota(jnp.int32, (HALF, count), 0).astype(F32)
    return pick, jnp.where(few == narrow, 1.0, 0.0)


def matrix_pick(table, rows, index):
    pick, mask = one_hots(index)
    spread = nn_dot(table, pick)
    low = rows * HALF
    return [
        jnp.sum(
            (spread[r * HALF : (r + 1) * HALF] + spread[low + r * HALF : low + (r + 1) * HALF]) * mask,
            axis=0,
            keepdims=True,
        )
        for r in range(rows)
    ]


def lane_pick(loads, blocks, index):
    lanes = jnp.broadcast_to(index & 127, (8, LANES))
    level = index >> 10
    spot = lax.broadcasted_iota(jnp.int32, (8, LANES), 0) == ((index >> 7) & 7)
    bits = []
    while 2 ** len(bits) < blocks:
        bits.append(jnp.broadcast_to((level & 2 ** len(bits)) != 0, (8, LANES)))

    def tree(load, first, depth):
        if depth == 0:
            return jnp.take_along_axis(load(first), lanes, axis=1, mode="promise_in_bounds")
        half = 2 ** (depth - 1)
        return jnp.where(
            bits[depth - 1], tree(load, first + half, depth - 1), tree(load, first, depth - 1)
        )

    return [
        jnp.sum(jnp.where(spot, tree(load, 0, len(bits)), 0.0), axis=0, keepdims=True) for load in loads
    ]


def put_into(rows, index):
    pick, mask = one_hots(index)
    mask = mask.astype(BF)
    parts = [two_parts(row) for row in rows]
    placed = nt_dot(jnp.concatenate([mask * part[k] for k in range(2) for part in parts], axis=0), pick)
    low = len(rows) * HALF
    return placed[:low] + placed[low:]


MESH = pl.DeviceIdType.MESH


def signal_all(barrier, cams, tiles):
    own_cam = lax.axis_index("cam")
    own_tile = lax.axis_index("tile")
    for step in range(cams):
        cam = lax.rem(own_cam + step, cams)

        def tell(i, carry, cam=cam):
            pl.semaphore_signal(
                barrier, inc=1, device_id=(cam, lax.rem(own_tile + i, tiles)), device_id_type=MESH
            )
            return carry

        lax.fori_loop(1 if step == 0 else 0, tiles, tell, 0, unroll=4)


def project_block(turn_ref, shift_ref, params_ref, table_ref, exact_ref, half, step, columns):
    rows = columns // LANES
    start = pl.multiple_of(half * (HALF * LANES) + step * columns, columns)
    params = []
    total = params_ref.shape[0]
    for first in range(0, total, 8):
        size = min(8, total - first)
        block = params_ref[first : first + size, pl.ds(start, columns)].reshape(size, rows, LANES)
        params.extend(block[r] for r in range(size))
    opacity = jax.nn.sigmoid(params[10])
    at = half * LANES
    place = pl.ds(pl.multiple_of(step * rows, rows), rows)
    far = pl.ds(pl.multiple_of(half * HALF + step * rows, rows), rows)
    for cam in range(4):
        matrix, eye = camera_of(turn_ref, shift_ref, cam, (rows, LANES))
        record = project(params, matrix, eye) + [opacity]
        for r, value in enumerate(record):
            if r in BY_LANES:
                exact_ref[cam, BY_LANES.index(r), far, :] = value
            else:
                value = jnp.where(value == value, jnp.clip(value, -BIG, BIG), 0.0)
                for k, part in enumerate(two_parts(value)):
                    table_ref[cam, k * len(BY_MATRIX) + BY_MATRIX.index(r), place, at : at + LANES] = part


def ask_kernel(
    cams, tiles, turn_ref, shift_ref, fetch_ref, params_ref, wanted_ref, table_ref, exact_ref,
    held_ref, send_sem, recv_sem, own_sem, load_sem,
):
    columns = 2048
    steps = HALF * LANES // columns
    load = pltpu.make_async_copy(params_ref, held_ref, load_sem)
    load.start()
    barrier = pltpu.get_barrier_semaphore()
    signal_all(barrier, cams, tiles)
    own_cam = lax.axis_index("cam")
    own_tile = lax.axis_index("tile")
    me = own_cam * tiles + own_tile
    others = cams * tiles - 1
    own = pltpu.make_async_copy(fetch_ref.at[me], wanted_ref.at[me], own_sem)
    own.start()
    pl.semaphore_wait(barrier, others)
    for hop in range(cams):
        cam = lax.rem(own_cam + hop, cams)

        def ask(i, carry, cam=cam):
            tile = lax.rem(own_tile + i, tiles)
            pltpu.make_async_remote_copy(
                src_ref=fetch_ref.at[cam * tiles + tile],
                dst_ref=wanted_ref.at[me],
                send_sem=send_sem,
                recv_sem=recv_sem,
                device_id=(cam, tile),
                device_id_type=MESH,
            ).start()
            return carry

        lax.fori_loop(1 if hop == 0 else 0, tiles, ask, 0, unroll=4)
    load.wait()

    def body(step, carry):
        for half in range(2):
            project_block(turn_ref, shift_ref, held_ref, table_ref, exact_ref, half, step, columns)
        return carry

    lax.fori_loop(0, steps, body, 0)
    own.wait()
    many = pl.ds(0, others)
    pltpu.make_async_copy(fetch_ref.at[many], wanted_ref.at[many], send_sem).wait()
    pltpu.make_async_copy(fetch_ref.at[many], wanted_ref.at[many], recv_sem).wait()


def ask_and_project(mesh_shape, fetch, splat_params, camera_turn, camera_shift):
    vmem = pl.BlockSpec(memory_space=pltpu.VMEM)
    smem = pl.BlockSpec(memory_space=pltpu.SMEM)
    return pl.pallas_call(
        functools.partial(ask_kernel, *mesh_shape),
        in_specs=[smem, smem, vmem, pl.BlockSpec(memory_space=pl.ANY)],
        out_specs=[vmem] * 3,
        out_shape=[
            jax.ShapeDtypeStruct(fetch.shape, jnp.int32),
            jax.ShapeDtypeStruct((4, 2 * len(BY_MATRIX), HALF, WIDE), BF),
            jax.ShapeDtypeStruct((4, len(BY_LANES), 2 * HALF, LANES), F32),
        ],
        scratch_shapes=[pltpu.VMEM(splat_params.shape, F32)] + [pltpu.SemaphoreType.DMA(())] * 4,
        compiler_params=pltpu.CompilerParams(
            vmem_limit_bytes=48 << 20, collective_id=0, has_side_effects=True
        ),
        name="ask_and_project",
    )(camera_turn, camera_shift, fetch, splat_params)


def pair_of(ref, chip):
    return jnp.concatenate([ref[2 * chip], ref[2 * chip + 1]], axis=1)


def answer_kernel(cams, tiles, wanted_ref, table_ref, exact_ref, got_ref, held_ref, send_sem, recv_sem, own_sem):
    chips = cams * tiles // 2
    per_cam = chips // cams
    others = 2 * chips - 1
    me = lax.axis_index("cam") * tiles + lax.axis_index("tile")
    own_chip = me // 2
    twin = 2 * own_chip + (1 - lax.rem(me, 2))
    barrier = pltpu.get_barrier_semaphore()
    signal_all(barrier, cams, tiles)

    def fill(chip):
        cam = chip // per_cam
        loads = [lambda v, r=r: exact_ref[cam, r, 8 * v : 8 * v + 8, :] for r in range(len(BY_LANES))]
        count = len(BY_MATRIX)
        middle = matrix_pick(
            table_ref[cam].reshape(2 * count * HALF, WIDE), count, pair_of(wanted_ref, chip)
        )
        for k in range(2):
            ends = lane_pick(loads, 2 * HALF // 8, wanted_ref[2 * chip + k])
            rows = [part[:, k * LANES : (k + 1) * LANES] for part in middle]
            held_ref[2 * chip + k, 0:9, :] = jnp.concatenate(ends[:2] + rows + ends[2:], axis=0)

    def send(other):
        pltpu.make_async_remote_copy(
            src_ref=held_ref.at[other, 0:9],
            dst_ref=got_ref.at[me, 0:9],
            send_sem=send_sem,
            recv_sem=recv_sem,
            device_id=(other // tiles, lax.rem(other, tiles)),
            device_id_type=MESH,
        ).start()

    per_batch = 4

    def fill_batch(batch):
        for k in range(per_batch):
            fill(lax.rem(own_chip + batch * per_batch + k, chips))

    def send_chip(step):
        chip = lax.rem(own_chip + step, chips)
        send(2 * chip)
        send(2 * chip + 1)

    fill_batch(0)
    own = pltpu.make_async_copy(held_ref.at[me, 0:9], got_ref.at[me, 0:9], own_sem)
    own.start()
    pl.semaphore_wait(barrier, others)
    send(twin)
    for k in range(1, per_batch):
        send_chip(k)

    def body(batch, carry):
        fill_batch(batch)
        for k in range(per_batch):
            send_chip(batch * per_batch + k)
        return carry

    lax.fori_loop(1, chips // per_batch, body, 0)
    own.wait()
    many = pl.ds(0, others)
    pltpu.make_async_copy(held_ref.at[many, 0:9], got_ref.at[many, 0:9], send_sem).wait()
    pltpu.make_async_copy(held_ref.at[many, 0:9], got_ref.at[many, 0:9], recv_sem).wait()


def answer(mesh_shape, wanted, table, exact):
    devices, _, capacity = wanted.shape
    shape = (devices, 16, capacity)
    return pl.pallas_call(
        functools.partial(answer_kernel, *mesh_shape),
        in_specs=[pl.BlockSpec(memory_space=pltpu.VMEM)] * 3,
        out_specs=pl.BlockSpec(memory_space=pltpu.VMEM),
        out_shape=jax.ShapeDtypeStruct(shape, F32),
        scratch_shapes=[pltpu.VMEM(shape, F32)] + [pltpu.SemaphoreType.DMA(())] * 3,
        compiler_params=pltpu.CompilerParams(
            vmem_limit_bytes=48 << 20, collective_id=1, has_side_effects=True
        ),
        name="answer",
    )(wanted, table, exact)


def render_kernel(
    counts_ref, ids_ref, got_ref, lists_ref, goal_ref, image_ref, grads_ref,
    table_ref, before_ref, after_ref, total_ref,
):
    tiles, entries = lists_ref.shape
    pixels = goal_ref.shape[2]

    for r in range(9):
        for i in range(0, 2 * HALF, 8):
            table_ref[r * 2 * HALF + i : r * 2 * HALF + i + 8, :] = got_ref[pl.ds(i * 16 + r, 8, stride=16), :]
    row = lax.broadcasted_iota(jnp.int32, (entries, entries), 0) & 127
    col = lax.broadcasted_iota(jnp.int32, (entries, entries), 1)
    before_ref[...] = jnp.where(row < col, 1.0, 0.0).astype(BF)
    after_ref[...] = jnp.where((row > col) | (col >= LANES), 1.0, 0.0).astype(BF)
    total_ref[...] = jnp.zeros_like(total_ref)

    def opening(tile):
        index = lists_ref[pl.ds(tile, 1), :]
        live = lax.broadcasted_iota(jnp.int32, (1, entries), 1) < counts_ref[0, tile]
        number = ids_ref[0, tile]
        origin_x = ((number & 31) * TILE_PX + TILE_PX // 2).astype(F32)
        origin_y = ((number >> 5) * TILE_PX + TILE_PX // 2).astype(F32)
        loads = [
            lambda v, r=r: table_ref[r * 2 * HALF + 8 * v : r * 2 * HALF + 8 * v + 8, :] for r in range(9)
        ]
        left = lane_pick(loads, 2 * HALF // 8, index[:, :LANES])
        right = lane_pick(loads, 2 * HALF // 8, index[:, LANES:])
        rec = [jnp.concatenate([left[r], right[r]], axis=1) for r in range(9)]
        rec_u = jnp.where(live, rec[0] - origin_x, 0.0)
        rec_v = jnp.where(live, rec[1] - origin_y, 0.0)
        con_a = jnp.where(live, rec[2], 0.0)
        con_b = jnp.where(live, rec[3], 0.0)
        con_c = jnp.where(live, rec[4], 0.0)
        log_o = jnp.where(live, jnp.maximum(jnp.log(rec[8]) * LOG2E, DEAD), DEAD)
        colours = [jnp.where(live, c, 0.0) for c in rec[5:8]]

        spot = lax.broadcasted_iota(jnp.int32, (TILE_PX, entries), 0).astype(F32) - 7.5
        off_x = spot - rec_u
        off_y = spot - rec_v
        part_x = (-0.5 * LOG2E) * con_a * off_x * off_x + log_o
        cross = (-LOG2E) * con_b * off_x
        part_y = (-0.5 * LOG2E) * con_c * off_y * off_y
        power = jnp.concatenate(
            [part_x + (cross * off_y[y : y + 1] + part_y[y : y + 1]) for y in range(TILE_PX)], axis=0
        )
        alphas = jnp.exp2(power)
        log_keep = jnp.log(jnp.maximum(1.0 - alphas, KEEP_MIN))
        return index, rec_u, rec_v, con_a, con_b, con_c, colours, power, alphas, log_keep

    def running(values, mask):
        parts = [two_parts(value) for value in values]
        sides = (slice(0, LANES), slice(LANES, 2 * LANES))
        stacked = [
            jnp.concatenate([part[0][:, side], part[1][:, side]], axis=1) for part in parts for side in sides
        ]
        sums = nn_dot(jnp.concatenate(stacked, axis=0), mask)
        rows = values[0].shape[0]
        return [
            [sums[(2 * t + h) * rows : (2 * t + h + 1) * rows] for h in range(2)] for t in range(len(values))
        ]

    def painting(tile, colours, ahead, alphas):
        weights = jnp.exp(ahead) * alphas
        w_high, w_low = two_parts(weights)

        col_parts = [two_parts(c) for c in colours]
        col_high = [p[0].astype(F32) for p in col_parts]
        col_low = [p[1].astype(F32) for p in col_parts]
        empty = [jnp.zeros((1, entries), F32)]
        col_stack = jnp.concatenate(col_high + col_low + empty * 10, axis=0).astype(BF)
        first = nt_dot(col_stack, w_high)
        second = nt_dot(col_stack, w_low)
        painted = [first[c : c + 1] + (first[3 + c : 4 + c] + second[c : c + 1]) for c in range(3)]
        residual = []
        for c in range(3):
            image_ref[c, pl.ds(tile, 1), :] = painted[c]
            residual.append(painted[c] - goal_ref[c, pl.ds(tile, 1), :])
        res_parts = [two_parts(c) for c in residual]
        res_high = [p[0].astype(F32) for p in res_parts]
        res_low = [p[1].astype(F32) for p in res_parts]
        blank = [jnp.zeros((1, pixels), F32)]
        res_left = jnp.concatenate(res_high + res_high + res_low + blank * 7, axis=0).astype(BF)
        col_right = jnp.concatenate(col_high + col_low + col_high + empty * 7, axis=0).astype(BF)
        weight_pull = tn_dot(res_left, col_right)
        res_stack = jnp.concatenate(res_high + res_low + blank * 10, axis=0).astype(BF)
        pull_one = nn_dot(res_stack, w_high)
        pull_two = nn_dot(res_stack, w_low)
        col_grads = [
            pull_one[c : c + 1] + (pull_one[3 + c : 4 + c] + pull_two[c : c + 1]) for c in range(3)
        ]
        share = weight_pull * weights
        return share, weights, col_grads

    def closing(tile, index, rec_u, rec_v, con_a, con_b, con_c, power, log_keep, share, behind, col_grads):
        spot = lax.broadcasted_iota(jnp.int32, (TILE_PX, entries), 0).astype(F32) - 7.5
        odds = jnp.exp2(power - log_keep * LOG2E)
        pull = share - odds * behind

        sum0 = jnp.zeros((TILE_PX, entries), F32)
        sum1 = sum0
        sum2 = sum0
        for y in range(TILE_PX - 1, -1, -1):
            sum0 = sum0 + pull[y * TILE_PX : (y + 1) * TILE_PX]
            sum1 = sum1 + sum0
            sum2 = sum2 + sum1
        first_y = sum1 - 8.5 * sum0
        second_y = 2.0 * sum2 - 18.0 * sum1 + 72.25 * sum0

        def over_x(value):
            return jnp.sum(value, axis=0, keepdims=True)

        m00 = over_x(sum0)
        m10 = over_x(spot * sum0)
        m20 = over_x(spot * spot * sum0)
        m01 = over_x(first_y)
        m11 = over_x(spot * first_y)
        m02 = over_x(second_y)
        by_x = m10 - rec_u * m00
        by_y = m01 - rec_v * m00
        by_xx = m20 - rec_u * (2.0 * m10 - rec_u * m00)
        by_xy = m11 - rec_u * m01 - rec_v * (m10 - rec_u * m00)
        by_yy = m02 - rec_v * (2.0 * m01 - rec_v * m00)
        grads = [
            con_a * by_x + con_b * by_y,
            con_c * by_y + con_b * by_x,
            -0.5 * by_xx,
            -by_xy,
            -0.5 * by_yy,
            col_grads[0],
            col_grads[1],
            col_grads[2],
            m00,
        ]
        total_ref[...] += put_into(grads, index)

    def tile_step(group):
        opened = [opening(tile) for tile in group]
        sums = running([o[9] for o in opened], before_ref[...])
        aheads = [
            jnp.concatenate([left[:, :LANES], right[:, :LANES] + left[:, LANES:]], axis=1)
            for left, right in sums
        ]
        painted = [painting(t, o[6], a, o[8]) for t, o, a in zip(group, opened, aheads)]
        sums = running([p[0] for p in painted], after_ref[...])
        behinds = [
            jnp.concatenate([left[:, :LANES] + right[:, LANES:], right[:, :LANES]], axis=1)
            for left, right in sums
        ]
        for t, o, p, b in zip(group, opened, painted, behinds):
            closing(t, *o[:6], o[7], o[9], p[0], b, p[2])

    per_step = 4

    def body(step, carry):
        tile_step([step * per_step + k for k in range(per_step)])
        return carry

    lax.fori_loop(0, tiles // per_step, body, 0)
    for h in range(2):
        for r in range(9):
            for i in range(0, HALF, 8):
                grads_ref[pl.ds((h * HALF + i) * 16 + r, 8, stride=16), :] = total_ref[
                    r * HALF + i : r * HALF + i + 8, h * LANES : (h + 1) * LANES
                ]


def render(counts, ids, got, lists, goal):
    tiles, entries = lists.shape
    vmem = pl.BlockSpec(memory_space=pltpu.VMEM)
    smem = pl.BlockSpec(memory_space=pltpu.SMEM)
    return pl.pallas_call(
        render_kernel,
        in_specs=[smem, smem, vmem, vmem, vmem],
        out_specs=[vmem, vmem],
        out_shape=[
            jax.ShapeDtypeStruct(goal.shape, F32),
            jax.ShapeDtypeStruct(got.shape, F32),
        ],
        scratch_shapes=[
            pltpu.VMEM((18 * HALF, LANES), F32),
            pltpu.VMEM((entries, entries), BF),
            pltpu.VMEM((entries, entries), BF),
            pltpu.VMEM((9 * HALF, WIDE), F32),
        ],
        compiler_params=pltpu.CompilerParams(vmem_limit_bytes=48 << 20),
        name="render",
    )(counts, ids, got, lists, goal)


def collect_kernel(
    cams, tiles, wanted_ref, away_ref, out_ref, back_ref, total_ref, send_sem, recv_sem
):
    chips = cams * tiles // 2
    per_cam = chips // cams
    per_group = 4
    groups = chips // per_group
    others = 2 * chips - 1
    me = lax.axis_index("cam") * tiles + lax.axis_index("tile")
    own_chip = me // 2
    twin = 2 * own_chip + (1 - lax.rem(me, 2))
    barrier = pltpu.get_barrier_semaphore()
    signal_all(barrier, cams, tiles)
    own = pltpu.make_async_copy(away_ref.at[me, 0:9], back_ref.at[me, 0:9], recv_sem.at[0])
    own.start()
    total_ref[...] = jnp.zeros_like(total_ref)
    pl.semaphore_wait(barrier, others)

    def send(other, group):
        pltpu.make_async_remote_copy(
            src_ref=away_ref.at[other, 0:9],
            dst_ref=back_ref.at[me, 0:9],
            send_sem=send_sem,
            recv_sem=recv_sem.at[group],
            device_id=(other // tiles, lax.rem(other, tiles)),
            device_id_type=MESH,
        ).start()

    send(twin, 0)

    def give(step, carry):
        chip = lax.rem(own_chip + step, chips)
        send(2 * chip, step // per_group)
        send(2 * chip + 1, step // per_group)
        return carry

    lax.fori_loop(1, chips, give, 0, unroll=3)

    def take(group, carry):
        block = pl.ds(0, 2 * per_group)
        pltpu.make_async_copy(away_ref.at[block, 0:9], back_ref.at[block, 0:9], recv_sem.at[group]).wait()
        for k in range(per_group):
            chip = lax.rem(own_chip + chips - (group * per_group + k), chips)
            both = jnp.concatenate([back_ref[2 * chip, 0:9, :], back_ref[2 * chip + 1, 0:9, :]], axis=1)
            viewer = jnp.full((1, WIDE), chip // per_cam, jnp.int32).astype(F32)
            rows = [both[r : r + 1] for r in range(9)] + [viewer]
            total_ref[...] += put_into(rows, pair_of(wanted_ref, chip))
        return carry

    lax.fori_loop(0, groups, take, 0)
    for r in range(10):
        for h in range(2):
            out_ref[r, h * HALF : (h + 1) * HALF, :] = total_ref[
                r * HALF : (r + 1) * HALF, h * LANES : (h + 1) * LANES
            ]
    many = pl.ds(0, others)
    pltpu.make_async_copy(away_ref.at[many, 0:9], back_ref.at[many, 0:9], send_sem).wait()


def collect(mesh_shape, wanted, away):
    chips = mesh_shape[0] * mesh_shape[1] // 2
    return pl.pallas_call(
        functools.partial(collect_kernel, *mesh_shape),
        in_specs=[pl.BlockSpec(memory_space=pltpu.VMEM)] * 2,
        out_specs=pl.BlockSpec(memory_space=pltpu.VMEM),
        out_shape=jax.ShapeDtypeStruct((10, 2 * HALF, LANES), F32),
        scratch_shapes=[
            pltpu.VMEM(away.shape, F32),
            pltpu.VMEM((10 * HALF, WIDE), F32),
            pltpu.SemaphoreType.DMA(()),
            pltpu.SemaphoreType.DMA((chips // 4,)),
        ],
        compiler_params=pltpu.CompilerParams(
            vmem_limit_bytes=48 << 20, collective_id=2, has_side_effects=True
        ),
        name="collect",
    )(wanted, away)


def step_size(row):
    if row < 3:
        return 0.00016
    if row < 6:
        return 0.005
    if row < 10:
        return 0.001
    if row < 11:
        return 0.025
    if row < 14:
        return 0.0025
    return 0.000125


def adam_kernel(turn_ref, shift_ref, pulls_ref, params_ref, one_ref, two_ref, new_ref, new_one_ref, new_two_ref):
    columns = params_ref.shape[1]
    total = params_ref.shape[0]
    rows = columns // LANES
    params = dense_rows(params_ref, columns)
    viewer = pulls_ref[9]
    matrix, eye = camera_of(turn_ref, shift_ref, 0, (rows, LANES))
    for cam in range(1, 4):
        here = viewer > cam - 0.5
        other, other_eye = camera_of(turn_ref, shift_ref, cam, (rows, LANES))
        matrix = [[jnp.where(here, other[i][j], matrix[i][j]) for j in range(3)] for i in range(3)]
        eye = [jnp.where(here, other_eye[i], eye[i]) for i in range(3)]
    _, pull_back = jax.vjp(lambda *values: project(values, matrix, eye), *params)
    grads = list(pull_back([pulls_ref[r] for r in range(8)]))
    grads[10] = pulls_ref[8] * jax.nn.sigmoid(-params[10])
    for start in range(0, total, 8):
        size = min(8, total - start)
        gradient = jnp.stack(grads[start : start + size], axis=0).reshape(size, columns)
        at = pl.ds(start, size)
        new_one = BETA_ONE * one_ref[at, :] + (1.0 - BETA_ONE) * gradient
        new_two = BETA_TWO * two_ref[at, :] + (1.0 - BETA_TWO) * gradient * gradient
        sizes = [step_size(row) / BIAS_ONE for row in range(start, start + size)]
        rate = jnp.full((size, 1), sizes[0], F32)
        which = lax.broadcasted_iota(jnp.int32, (size, 1), 0)
        for k in range(1, size):
            if sizes[k] != sizes[k - 1]:
                rate = jnp.where(which >= k, sizes[k], rate)
        new_one_ref[at, :] = new_one
        new_two_ref[at, :] = new_two
        new_ref[at, :] = params_ref[at, :] - rate * new_one / (
            jnp.sqrt(new_two * (1.0 / BIAS_TWO)) + ADAM_EPS
        )


def apply_adam(pulls, params, one, two, camera_turn, camera_shift):
    rows_in, own_count = params.shape
    columns = 1024
    block = pl.BlockSpec((rows_in, columns), lambda i: (0, i))
    return pl.pallas_call(
        adam_kernel,
        grid=(own_count // columns,),
        in_specs=[
            pl.BlockSpec(memory_space=pltpu.SMEM),
            pl.BlockSpec(memory_space=pltpu.SMEM),
            pl.BlockSpec((10, columns // LANES, LANES), lambda i: (0, i, 0)),
            block,
            block,
            block,
        ],
        out_specs=[block] * 3,
        out_shape=[jax.ShapeDtypeStruct(params.shape, F32)] * 3,
        compiler_params=pltpu.CompilerParams(vmem_limit_bytes=48 << 20),
        name="apply_adam",
    )(camera_turn, camera_shift, pulls, params, one, two)


def shards(
    splat_params,
    first_moment,
    second_moment,
    camera_turn,
    camera_shift,
    fetch_table,
    tile_lists,
    tile_counts,
    tile_ids,
    target_image,
):
    devices, capacity = fetch_table.shape[1:]
    mesh_shape = (lax.axis_size("cam"), lax.axis_size("tile"))
    wanted, table, exact = ask_and_project(
        mesh_shape, fetch_table.reshape(devices, 1, capacity), splat_params, camera_turn, camera_shift
    )
    arrived = answer(mesh_shape, wanted, table, exact)
    rendered, slot_grads = render(
        tile_counts, tile_ids, arrived.reshape(devices * 16, capacity), tile_lists[0], target_image[:, 0]
    )
    pulls = collect(mesh_shape, wanted, slot_grads.reshape(devices, 16, capacity))
    updated_params, updated_first, updated_second = apply_adam(
        pulls, splat_params, first_moment, second_moment, camera_turn, camera_shift
    )
    return (updated_params, updated_first, updated_second, rendered[:, None])


def solution(mesh):
    return jax.shard_map(
        shards,
        mesh=mesh,
        in_specs=(
            P(None, ("cam", "tile")),
            P(None, ("cam", "tile")),
            P(None, ("cam", "tile")),
            P(),
            P(),
            P(("cam", "tile"), None, None),
            P("cam", "tile", None),
            P("cam", "tile"),
            P("cam", "tile"),
            P(None, "cam", "tile", None),
        ),
        out_specs=(
            P(None, ("cam", "tile")),
            P(None, ("cam", "tile")),
            P(None, ("cam", "tile")),
            P(None, "cam", "tile", None),
        ),
        check_vma=False,
    )
```

```python
import functools
import math

import jax
import jax.numpy as jnp
from jax import lax
from jax.experimental import pallas as pl
from jax.experimental.pallas import tpu as pltpu
from jax.sharding import PartitionSpec as P

TILE_PX = 16
GRID = 32


FOCAL = 512.0
CENTRE = 256.0
EYE_GAP = 20.0
DILATION = 0.3
SH_ZERO = 0.28209479177387814
SH_ONE = 0.4886025119029199
SH_TWO = (
    1.0925484305920792,
    -1.0925484305920792,
    0.31539156525252005,
    -1.0925484305920792,
    0.5462742152960396,
)
SH_THREE = (
    -0.5900435899266435,
    2.890611442640554,
    -0.4570457994644658,
    0.3731763325901154,
    -0.4570457994644658,
    1.445305721320277,
    -0.5900435899266435,
)
BETA_ONE = 0.9
BETA_TWO = 0.999
BIAS_ONE = 1.0 - math.exp(2000.0 * math.log(0.9))
BIAS_TWO = 1.0 - math.exp(2000.0 * math.log(0.999))
ADAM_EPS = 1e-08


def harmonics(dir_x, dir_y, dir_z):
    sq_x = dir_x * dir_x
    sq_y = dir_y * dir_y
    sq_z = dir_z * dir_z
    return [
        SH_ZERO * jnp.ones_like(dir_x),
        -SH_ONE * dir_y,
        SH_ONE * dir_z,
        -SH_ONE * dir_x,
        SH_TWO[0] * dir_x * dir_y,
        SH_TWO[1] * dir_y * dir_z,
        SH_TWO[2] * (2.0 * sq_z - sq_x - sq_y),
        SH_TWO[3] * dir_x * dir_z,
        SH_TWO[4] * (sq_x - sq_y),
        SH_THREE[0] * dir_y * (3.0 * sq_x - sq_y),
        SH_THREE[1] * dir_x * dir_y * dir_z,
        SH_THREE[2] * dir_y * (4.0 * sq_z - sq_x - sq_y),
        SH_THREE[3] * dir_z * (2.0 * sq_z - 3.0 * sq_x - 3.0 * sq_y),
        SH_THREE[4] * dir_x * (4.0 * sq_z - sq_x - sq_y),
        SH_THREE[5] * dir_z * (sq_x - sq_y),
        SH_THREE[6] * dir_x * (sq_x - 3.0 * sq_y),
    ]


def quat_matrix(quat_w, quat_x, quat_y, quat_z):
    return [
        [
            1.0 - 2.0 * (quat_y * quat_y + quat_z * quat_z),
            2.0 * (quat_x * quat_y - quat_w * quat_z),
            2.0 * (quat_x * quat_z + quat_w * quat_y),
        ],
        [
            2.0 * (quat_x * quat_y + quat_w * quat_z),
            1.0 - 2.0 * (quat_x * quat_x + quat_z * quat_z),
            2.0 * (quat_y * quat_z - quat_w * quat_x),
        ],
        [
            2.0 * (quat_x * quat_z - quat_w * quat_y),
            2.0 * (quat_y * quat_z + quat_w * quat_x),
            1.0 - 2.0 * (quat_x * quat_x + quat_y * quat_y),
        ],
    ]

LOG2E = math.log2(math.e)
HALF = 64
WIDE = 256
LANES = 128
BIG = 3e38
BY_LANES = (0, 1, 8)
BY_MATRIX = (2, 3, 4, 5, 6, 7)
DEAD = -1e4
KEEP_MIN = 2.0**-24
EARLY_STEPS = 2
BF = jnp.bfloat16
F32 = jnp.float32


@jax.custom_vjp
def inverse(value):
    return 1.0 / value


def inverse_fwd(value):
    result = 1.0 / value
    return result, result


def inverse_bwd(result, pull):
    return (-pull * result * result,)


inverse.defvjp(inverse_fwd, inverse_bwd)


@jax.custom_vjp
def inverse_root(value):
    return 1.0 / jnp.sqrt(value)


def inverse_root_fwd(value):
    result = 1.0 / jnp.sqrt(value)
    return result, result


def inverse_root_bwd(result, pull):
    return (-0.5 * pull * result * (result * result),)


inverse_root.defvjp(inverse_root_fwd, inverse_root_bwd)


def project(params, camera, eye_pos):
    scales = [jnp.exp(params[3 + i]) for i in range(3)]
    inv_norm = inverse_root(
        params[6] * params[6]
        + params[7] * params[7]
        + params[8] * params[8]
        + params[9] * params[9]
    )
    rotation = quat_matrix(
        params[6] * inv_norm, params[7] * inv_norm, params[8] * inv_norm, params[9] * inv_norm
    )
    relative = [params[i] - eye_pos[i] for i in range(3)]
    in_view = [
        camera[i][0] * relative[0] + camera[i][1] * relative[1] + camera[i][2] * relative[2]
        for i in range(3)
    ]
    inv_depth = inverse(in_view[2])
    screen_x = FOCAL * in_view[0] * inv_depth + CENTRE
    screen_y = FOCAL * in_view[1] * inv_depth + CENTRE
    axes_cam = [
        [
            (
                camera[i][0] * rotation[0][k]
                + camera[i][1] * rotation[1][k]
                + camera[i][2] * rotation[2][k]
            )
            * scales[k]
            for k in range(3)
        ]
        for i in range(3)
    ]
    slope_x = FOCAL * in_view[0] * inv_depth * inv_depth
    slope_y = FOCAL * in_view[1] * inv_depth * inv_depth
    row_x = [FOCAL * inv_depth * axes_cam[0][k] - slope_x * axes_cam[2][k] for k in range(3)]
    row_y = [FOCAL * inv_depth * axes_cam[1][k] - slope_y * axes_cam[2][k] for k in range(3)]
    cov_xx = row_x[0] * row_x[0] + row_x[1] * row_x[1] + row_x[2] * row_x[2] + DILATION
    cov_xy = row_x[0] * row_y[0] + row_x[1] * row_y[1] + row_x[2] * row_y[2]
    cov_yy = row_y[0] * row_y[0] + row_y[1] * row_y[1] + row_y[2] * row_y[2] + DILATION
    inv_det = inverse(cov_xx * cov_yy - cov_xy * cov_xy)
    inv_dist = inverse_root(
        relative[0] * relative[0] + relative[1] * relative[1] + relative[2] * relative[2]
    )
    basis = harmonics(relative[0] * inv_dist, relative[1] * inv_dist, relative[2] * inv_dist)
    colours = []
    for channel in range(3):
        total = basis[0] * params[11 + channel]
        for k in range(1, 16):
            total = total + basis[k] * params[11 + 3 * k + channel]
        colours.append(jnp.maximum(total + 0.5, 0.0))
    return [
        screen_x,
        screen_y,
        cov_yy * inv_det,
        -cov_xy * inv_det,
        cov_xx * inv_det,
        colours[0],
        colours[1],
        colours[2],
    ]


def camera_of(turn_ref, shift_ref, cam, shape):
    turn = [jnp.full(shape, turn_ref[cam, i], F32) for i in range(3)]
    norm = jnp.sqrt(1.0 + (turn[0] * turn[0] + turn[1] * turn[1] + turn[2] * turn[2]))
    matrix = quat_matrix(1.0 / norm, turn[0] / norm, turn[1] / norm, turn[2] / norm)
    eye = [jnp.full(shape, shift_ref[cam, i], F32) for i in range(3)]
    eye[0] = EYE_GAP * cam + eye[0]
    return matrix, eye


def dense_rows(ref, columns):
    rows = []
    total = ref.shape[0]
    for start in range(0, total, 8):
        size = min(8, total - start)
        block = ref[start : start + size, :].reshape(size, columns // LANES, LANES)
        rows.extend(block[r] for r in range(size))
    return rows


def two_parts(value):
    high = value.astype(BF)
    return high, (value - high.astype(F32)).astype(BF)


def nt_dot(lhs, rhs):
    return lax.dot_general(lhs, rhs, (((1,), (1,)), ((), ())), preferred_element_type=F32)


def tn_dot(lhs, rhs):
    return lax.dot_general(lhs, rhs, (((0,), (0,)), ((), ())), preferred_element_type=F32)


def nn_dot(lhs, rhs):
    return lax.dot_general(lhs, rhs, (((1,), (0,)), ((), ())), preferred_element_type=F32)


def one_hots(index):
    count = index.shape[1]
    wide = ((index >> 13) * LANES + (index & 127)).astype(F32).astype(BF)
    narrow = ((index >> 7) & 63).astype(F32)
    one = jnp.ones((), BF)
    zero = jnp.zeros((), BF)
    rows = lax.broadcasted_iota(jnp.int32, (WIDE, count), 0).astype(F32).astype(BF)
    pick = jnp.where(rows == wide, one, zero)
    few = lax.broadcasted_iota(jnp.int32, (HALF, count), 0).astype(F32)
    return pick, jnp.where(few == narrow, 1.0, 0.0)


def matrix_pick(table, rows, index):
    pick, mask = one_hots(index)
    spread = nn_dot(table, pick)
    low = rows * HALF
    return [
        jnp.sum(
            (spread[r * HALF : (r + 1) * HALF] + spread[low + r * HALF : low + (r + 1) * HALF]) * mask,
            axis=0,
            keepdims=True,
        )
        for r in range(rows)
    ]


def lane_pick(loads, blocks, index):
    lanes = jnp.broadcast_to(index & 127, (8, LANES))
    level = index >> 10
    spot = lax.broadcasted_iota(jnp.int32, (8, LANES), 0) == ((index >> 7) & 7)
    bits = []
    while 2 ** len(bits) < blocks:
        bits.append(jnp.broadcast_to((level & 2 ** len(bits)) != 0, (8, LANES)))

    def tree(load, first, depth):
        if depth == 0:
            return jnp.take_along_axis(load(first), lanes, axis=1, mode="promise_in_bounds")
        half = 2 ** (depth - 1)
        return jnp.where(
            bits[depth - 1], tree(load, first + half, depth - 1), tree(load, first, depth - 1)
        )

    return [
        jnp.sum(jnp.where(spot, tree(load, 0, len(bits)), 0.0), axis=0, keepdims=True) for load in loads
    ]


def put_into(rows, index):
    pick, mask = one_hots(index)
    mask = mask.astype(BF)
    parts = [two_parts(row) for row in rows]
    placed = nt_dot(jnp.concatenate([mask * part[k] for k in range(2) for part in parts], axis=0), pick)
    low = len(rows) * HALF
    return placed[:low] + placed[low:]


MESH = pl.DeviceIdType.MESH


def signal_all(barrier, cams, tiles):
    own_cam = lax.axis_index("cam")
    own_tile = lax.axis_index("tile")
    for step in range(cams):
        cam = lax.rem(own_cam + step, cams)

        def tell(i, carry, cam=cam):
            pl.semaphore_signal(
                barrier, inc=1, device_id=(cam, lax.rem(own_tile + i, tiles)), device_id_type=MESH
            )
            return carry

        lax.fori_loop(1 if step == 0 else 0, tiles, tell, 0, unroll=4)


def project_block(turn_ref, shift_ref, params_ref, table_ref, exact_ref, half, step, columns):
    rows = columns // LANES
    start = pl.multiple_of(half * (HALF * LANES) + step * columns, columns)
    params = []
    total = params_ref.shape[0]
    for first in range(0, total, 8):
        size = min(8, total - first)
        block = params_ref[first : first + size, pl.ds(start, columns)].reshape(size, rows, LANES)
        params.extend(block[r] for r in range(size))
    opacity = jax.nn.sigmoid(params[10])
    at = half * LANES
    place = pl.ds(pl.multiple_of(step * rows, rows), rows)
    far = pl.ds(pl.multiple_of(half * HALF + step * rows, rows), rows)
    for cam in range(4):
        matrix, eye = camera_of(turn_ref, shift_ref, cam, (rows, LANES))
        record = project(params, matrix, eye) + [opacity]
        for r, value in enumerate(record):
            if r in BY_LANES:
                exact_ref[cam, BY_LANES.index(r), far, :] = value
            else:
                value = jnp.where(value == value, jnp.clip(value, -BIG, BIG), 0.0)
                for k, part in enumerate(two_parts(value)):
                    table_ref[cam, k * len(BY_MATRIX) + BY_MATRIX.index(r), place, at : at + LANES] = part


def ask_phase(cams, tiles, turn_ref, shift_ref, fetch_ref, params_ref, wanted_ref, table_ref, exact_ref,
              ready, send_sem, recv_sem, own_sem):
    columns = 2048
    steps = HALF * LANES // columns
    barrier = pltpu.get_barrier_semaphore()
    signal_all(barrier, cams, tiles)
    own_cam = lax.axis_index("cam")
    own_tile = lax.axis_index("tile")
    me = own_cam * tiles + own_tile
    others = cams * tiles - 1
    own = pltpu.make_async_copy(fetch_ref.at[me], wanted_ref.at[me], own_sem)
    own.start()
    for copy in ready:
        copy.wait()

    def body(step, carry):
        for half in range(2):
            project_block(turn_ref, shift_ref, params_ref, table_ref, exact_ref, half, step, columns)
        return carry

    early = EARLY_STEPS
    lax.fori_loop(0, early, body, 0)
    pl.semaphore_wait(barrier, others)
    for hop in range(cams):
        cam = lax.rem(own_cam + hop, cams)

        def ask(i, carry, cam=cam):
            tile = lax.rem(own_tile + i, tiles)
            pltpu.make_async_remote_copy(
                src_ref=fetch_ref.at[cam * tiles + tile],
                dst_ref=wanted_ref.at[me],
                send_sem=send_sem,
                recv_sem=recv_sem,
                device_id=(cam, tile),
                device_id_type=MESH,
            ).start()
            return carry

        lax.fori_loop(1 if hop == 0 else 0, tiles, ask, 0, unroll=4)
    lax.fori_loop(early, steps, body, 0)
    own.wait()
    many = pl.ds(0, others)
    pltpu.make_async_copy(fetch_ref.at[many], wanted_ref.at[many], send_sem).wait()
    pltpu.make_async_copy(fetch_ref.at[many], wanted_ref.at[many], recv_sem).wait()


def pair_of(ref, chip):
    return jnp.concatenate([ref[2 * chip], ref[2 * chip + 1]], axis=1)


def answer_phase(cams, tiles, wanted_ref, table_ref, exact_ref, got_ref, held_ref, send_sem, recv_sem, own_sem):
    chips = cams * tiles // 2
    per_cam = chips // cams
    others = 2 * chips - 1
    me = lax.axis_index("cam") * tiles + lax.axis_index("tile")
    own_chip = me // 2
    twin = 2 * own_chip + (1 - lax.rem(me, 2))

    def fill(chip):
        cam = chip // per_cam
        loads = [lambda v, r=r: exact_ref[cam, r, 8 * v : 8 * v + 8, :] for r in range(len(BY_LANES))]
        count = len(BY_MATRIX)
        middle = matrix_pick(
            table_ref[cam].reshape(2 * count * HALF, WIDE), count, pair_of(wanted_ref, chip)
        )
        for k in range(2):
            ends = lane_pick(loads, 2 * HALF // 8, wanted_ref[2 * chip + k])
            rows = [part[:, k * LANES : (k + 1) * LANES] for part in middle]
            held_ref[2 * chip + k, 0:9, :] = jnp.concatenate(ends[:2] + rows + ends[2:], axis=0)

    def send(other):
        pltpu.make_async_remote_copy(
            src_ref=held_ref.at[other, 0:9],
            dst_ref=got_ref.at[me, 0:9],
            send_sem=send_sem,
            recv_sem=recv_sem,
            device_id=(other // tiles, lax.rem(other, tiles)),
            device_id_type=MESH,
        ).start()

    per_batch = 4

    def fill_batch(batch):
        for k in range(per_batch):
            fill(lax.rem(own_chip + batch * per_batch + k, chips))

    def send_chip(step):
        chip = lax.rem(own_chip + step, chips)
        send(2 * chip)
        send(2 * chip + 1)

    fill_batch(0)
    own = pltpu.make_async_copy(held_ref.at[me, 0:9], got_ref.at[me, 0:9], own_sem)
    own.start()
    send(twin)
    for k in range(1, per_batch):
        send_chip(k)

    def body(batch, carry):
        fill_batch(batch)
        for k in range(per_batch):
            send_chip(batch * per_batch + k)
        return carry

    lax.fori_loop(1, chips // per_batch, body, 0)
    own.wait()
    many = pl.ds(0, others)
    pltpu.make_async_copy(held_ref.at[many, 0:9], got_ref.at[many, 0:9], send_sem).wait()
    pltpu.make_async_copy(held_ref.at[many, 0:9], got_ref.at[many, 0:9], recv_sem).wait()


def render_phase(
    counts_ref, ids_ref, got_ref, lists_ref, goal_ref, image_ref, grads_ref,
    table_ref, before_ref, after_ref, total_ref,
):
    tiles, entries = lists_ref.shape
    pixels = goal_ref.shape[2]

    for r in range(9):
        for i in range(0, 2 * HALF, 8):
            table_ref[r * 2 * HALF + i : r * 2 * HALF + i + 8, :] = jnp.concatenate([got_ref[i + k, r : r + 1, :] for k in range(8)], axis=0)
    row = lax.broadcasted_iota(jnp.int32, (entries, entries), 0) & 127
    col = lax.broadcasted_iota(jnp.int32, (entries, entries), 1)
    before_ref[...] = jnp.where(row < col, 1.0, 0.0).astype(BF)
    after_ref[...] = jnp.where((row > col) | (col >= LANES), 1.0, 0.0).astype(BF)
    total_ref[...] = jnp.zeros_like(total_ref)

    def opening(tile):
        index = lists_ref[pl.ds(tile, 1), :]
        live = lax.broadcasted_iota(jnp.int32, (1, entries), 1) < counts_ref[0, tile]
        number = ids_ref[0, tile]
        origin_x = ((number & 31) * TILE_PX + TILE_PX // 2).astype(F32)
        origin_y = ((number >> 5) * TILE_PX + TILE_PX // 2).astype(F32)
        loads = [
            lambda v, r=r: table_ref[r * 2 * HALF + 8 * v : r * 2 * HALF + 8 * v + 8, :] for r in range(9)
        ]
        left = lane_pick(loads, 2 * HALF // 8, index[:, :LANES])
        right = lane_pick(loads, 2 * HALF // 8, index[:, LANES:])
        rec = [jnp.concatenate([left[r], right[r]], axis=1) for r in range(9)]
        rec_u = jnp.where(live, rec[0] - origin_x, 0.0)
        rec_v = jnp.where(live, rec[1] - origin_y, 0.0)
        con_a = jnp.where(live, rec[2], 0.0)
        con_b = jnp.where(live, rec[3], 0.0)
        con_c = jnp.where(live, rec[4], 0.0)
        log_o = jnp.where(live, jnp.maximum(jnp.log(rec[8]) * LOG2E, DEAD), DEAD)
        colours = [jnp.where(live, c, 0.0) for c in rec[5:8]]

        spot = lax.broadcasted_iota(jnp.int32, (TILE_PX, entries), 0).astype(F32) - 7.5
        off_x = spot - rec_u
        off_y = spot - rec_v
        part_x = (-0.5 * LOG2E) * con_a * off_x * off_x + log_o
        cross = (-LOG2E) * con_b * off_x
        part_y = (-0.5 * LOG2E) * con_c * off_y * off_y
        power = jnp.concatenate(
            [part_x + (cross * off_y[y : y + 1] + part_y[y : y + 1]) for y in range(TILE_PX)], axis=0
        )
        alphas = jnp.exp2(power)
        log_keep = jnp.log(jnp.maximum(1.0 - alphas, KEEP_MIN))
        return index, rec_u, rec_v, con_a, con_b, con_c, colours, power, alphas, log_keep

    def running(values, mask):
        parts = [two_parts(value) for value in values]
        sides = (slice(0, LANES), slice(LANES, 2 * LANES))
        stacked = [
            jnp.concatenate([part[0][:, side], part[1][:, side]], axis=1) for part in parts for side in sides
        ]
        sums = nn_dot(jnp.concatenate(stacked, axis=0), mask)
        rows = values[0].shape[0]
        return [
            [sums[(2 * t + h) * rows : (2 * t + h + 1) * rows] for h in range(2)] for t in range(len(values))
        ]

    def painting(tile, colours, ahead, alphas):
        weights = jnp.exp(ahead) * alphas
        w_high, w_low = two_parts(weights)

        col_parts = [two_parts(c) for c in colours]
        col_high = [p[0].astype(F32) for p in col_parts]
        col_low = [p[1].astype(F32) for p in col_parts]
        empty = [jnp.zeros((1, entries), F32)]
        col_stack = jnp.concatenate(col_high + col_low + empty * 10, axis=0).astype(BF)
        first = nt_dot(col_stack, w_high)
        second = nt_dot(col_stack, w_low)
        painted = [first[c : c + 1] + (first[3 + c : 4 + c] + second[c : c + 1]) for c in range(3)]
        residual = []
        for c in range(3):
            image_ref[c, pl.ds(tile, 1), :] = painted[c]
            residual.append(painted[c] - goal_ref[c, pl.ds(tile, 1), :])
        res_parts = [two_parts(c) for c in residual]
        res_high = [p[0].astype(F32) for p in res_parts]
        res_low = [p[1].astype(F32) for p in res_parts]
        blank = [jnp.zeros((1, pixels), F32)]
        res_left = jnp.concatenate(res_high + res_high + res_low + blank * 7, axis=0).astype(BF)
        col_right = jnp.concatenate(col_high + col_low + col_high + empty * 7, axis=0).astype(BF)
        weight_pull = tn_dot(res_left, col_right)
        res_stack = jnp.concatenate(res_high + res_low + blank * 10, axis=0).astype(BF)
        pull_one = nn_dot(res_stack, w_high)
        pull_two = nn_dot(res_stack, w_low)
        col_grads = [
            pull_one[c : c + 1] + (pull_one[3 + c : 4 + c] + pull_two[c : c + 1]) for c in range(3)
        ]
        share = weight_pull * weights
        return share, weights, col_grads

    def closing(tile, index, rec_u, rec_v, con_a, con_b, con_c, power, log_keep, share, behind, col_grads):
        spot = lax.broadcasted_iota(jnp.int32, (TILE_PX, entries), 0).astype(F32) - 7.5
        odds = jnp.exp2(power - log_keep * LOG2E)
        pull = share - odds * behind

        sum0 = jnp.zeros((TILE_PX, entries), F32)
        sum1 = sum0
        sum2 = sum0
        for y in range(TILE_PX - 1, -1, -1):
            sum0 = sum0 + pull[y * TILE_PX : (y + 1) * TILE_PX]
            sum1 = sum1 + sum0
            sum2 = sum2 + sum1
        first_y = sum1 - 8.5 * sum0
        second_y = 2.0 * sum2 - 18.0 * sum1 + 72.25 * sum0

        def over_x(value):
            return jnp.sum(value, axis=0, keepdims=True)

        m00 = over_x(sum0)
        m10 = over_x(spot * sum0)
        m20 = over_x(spot * spot * sum0)
        m01 = over_x(first_y)
        m11 = over_x(spot * first_y)
        m02 = over_x(second_y)
        by_x = m10 - rec_u * m00
        by_y = m01 - rec_v * m00
        by_xx = m20 - rec_u * (2.0 * m10 - rec_u * m00)
        by_xy = m11 - rec_u * m01 - rec_v * (m10 - rec_u * m00)
        by_yy = m02 - rec_v * (2.0 * m01 - rec_v * m00)
        grads = [
            con_a * by_x + con_b * by_y,
            con_c * by_y + con_b * by_x,
            -0.5 * by_xx,
            -by_xy,
            -0.5 * by_yy,
            col_grads[0],
            col_grads[1],
            col_grads[2],
            m00,
        ]
        total_ref[...] += put_into(grads, index)

    def tile_step(group):
        opened = [opening(tile) for tile in group]
        sums = running([o[9] for o in opened], before_ref[...])
        aheads = [
            jnp.concatenate([left[:, :LANES], right[:, :LANES] + left[:, LANES:]], axis=1)
            for left, right in sums
        ]
        painted = [painting(t, o[6], a, o[8]) for t, o, a in zip(group, opened, aheads)]
        sums = running([p[0] for p in painted], after_ref[...])
        behinds = [
            jnp.concatenate([left[:, :LANES] + right[:, LANES:], right[:, :LANES]], axis=1)
            for left, right in sums
        ]
        for t, o, p, b in zip(group, opened, painted, behinds):
            closing(t, *o[:6], o[7], o[9], p[0], b, p[2])

    per_step = 16

    def body(step, carry):
        tile_step([step * per_step + k for k in range(per_step)])
        return carry

    lax.fori_loop(0, tiles // per_step, body, 0)
    def lay(step, carry):
        start = pl.multiple_of(8 * step, 8)
        for h in range(2):
            block = [
                total_ref[pl.ds(pl.multiple_of(r * HALF + start, 8), 8), h * LANES : (h + 1) * LANES]
                for r in range(9)
            ]
            for k in range(8):
                grads_ref[h * HALF + start + k, 0:9, :] = jnp.concatenate(
                    [part[k : k + 1] for part in block], axis=0
                )
        return carry

    lax.fori_loop(0, HALF // 8, lay, 0)


def collect_phase(
    cams, tiles, wanted_ref, away_ref, out_ref, back_ref, total_ref, send_sem, recv_sem, own_sem
):
    chips = cams * tiles // 2
    per_cam = chips // cams
    per_group = 8
    groups = chips // per_group
    ahead = 2
    others = 2 * chips - 1
    me = lax.axis_index("cam") * tiles + lax.axis_index("tile")
    own_chip = me // 2
    twin = 2 * own_chip + (1 - lax.rem(me, 2))
    own = pltpu.make_async_copy(away_ref.at[me, 0:9], back_ref.at[me, 0:9], own_sem)
    own.start()

    def send(other, group):
        pltpu.make_async_remote_copy(
            src_ref=away_ref.at[other, 0:9],
            dst_ref=back_ref.at[me, 0:9],
            send_sem=send_sem,
            recv_sem=recv_sem.at[group],
            device_id=(other // tiles, lax.rem(other, tiles)),
            device_id_type=MESH,
        ).start()

    def send_group(group, first):
        for k in range(first, per_group):
            chip = lax.rem(own_chip + group * per_group + k, chips)
            send(2 * chip, group)
            send(2 * chip + 1, group)

    send(twin, 0)
    send_group(0, 1)
    for group in range(1, ahead):
        send_group(group, 0)
    total_ref[...] = jnp.zeros_like(total_ref)
    own.wait()

    def add_group(group):
        for k in range(per_group):
            chip = lax.rem(own_chip + chips - (group * per_group + k), chips)
            both = jnp.concatenate([back_ref[2 * chip, 0:9, :], back_ref[2 * chip + 1, 0:9, :]], axis=1)
            viewer = jnp.full((1, WIDE), chip // per_cam, jnp.int32).astype(F32)
            rows = [both[r : r + 1] for r in range(9)] + [viewer]
            total_ref[...] += put_into(rows, pair_of(wanted_ref, chip))

    def arrive(group, count):
        block = pl.ds(0, count)
        pltpu.make_async_copy(away_ref.at[block, 0:9], back_ref.at[block, 0:9], recv_sem.at[group]).wait()

    def take_and_send(group, carry):
        send_group(group + ahead, 0)
        arrive(group, 2 * per_group)
        add_group(group)
        return carry

    def take(group, carry):
        arrive(group, 2 * per_group)
        add_group(group)
        return carry

    arrive(0, 2 * per_group - 1)
    send_group(ahead, 0)
    add_group(0)
    lax.fori_loop(1, groups - ahead, take_and_send, 0)
    lax.fori_loop(groups - ahead, groups, take, 0)
    for r in range(10):
        for h in range(2):
            out_ref[r, h * HALF : (h + 1) * HALF, :] = total_ref[
                r * HALF : (r + 1) * HALF, h * LANES : (h + 1) * LANES
            ]
    many = pl.ds(0, others)
    pltpu.make_async_copy(away_ref.at[many, 0:9], back_ref.at[many, 0:9], send_sem).wait()


def work_kernel(
    cams, tiles, turn_hbm, shift_hbm, counts_hbm, ids_hbm, fetch_hbm, params_hbm, lists_hbm, goal_hbm,
    image_ref, pulls_ref,
    turn_ref, shift_ref, counts_ref, ids_ref, params_ref, lists_ref, goal_ref,
    wanted_ref, table_ref, exact_ref, held_ref, got_ref, spread_ref, before_ref, after_ref, slots_ref,
    away_ref, back_ref, total_ref, load_sems, send_sems, recv_sems, own_sems, group_sems,
):
    loads = [
        pltpu.make_async_copy(source, target, load_sems.at[k])
        for k, (source, target) in enumerate(
            [
                (params_hbm, params_ref),
                (turn_hbm, turn_ref),
                (shift_hbm, shift_ref),
                (counts_hbm, counts_ref),
                (ids_hbm, ids_ref),
                (lists_hbm, lists_ref),
                (goal_hbm, goal_ref),
            ]
        )
    ]
    for load in loads:
        load.start()
    ask_phase(
        cams, tiles, turn_ref, shift_ref, fetch_hbm, params_ref, wanted_ref, table_ref, exact_ref,
        loads[:3], send_sems.at[0], recv_sems.at[0], own_sems.at[0],
    )
    answer_phase(
        cams, tiles, wanted_ref, table_ref, exact_ref, got_ref, held_ref,
        send_sems.at[1], recv_sems.at[1], own_sems.at[1],
    )
    for load in loads[3:]:
        load.wait()
    render_phase(
        counts_ref, ids_ref, got_ref, lists_ref, goal_ref, image_ref, away_ref,
        spread_ref, before_ref, after_ref, slots_ref,
    )
    collect_phase(
        cams, tiles, wanted_ref, away_ref, pulls_ref, back_ref, total_ref,
        send_sems.at[2], group_sems, own_sems.at[2],
    )


def work(mesh_shape, turn, shift, counts, ids, fetch, params, lists, goal):
    devices, _, capacity = fetch.shape
    entries = lists.shape[1]
    hbm = pl.BlockSpec(memory_space=pltpu.HBM)
    vmem = pl.BlockSpec(memory_space=pltpu.VMEM)
    blocks = pltpu.VMEM((devices, 16, capacity), F32)
    return pl.pallas_call(
        functools.partial(work_kernel, *mesh_shape),
        in_specs=[hbm] * 8,
        out_specs=[vmem] * 2,
        out_shape=[
            jax.ShapeDtypeStruct(goal.shape, F32),
            jax.ShapeDtypeStruct((10, 2 * HALF, LANES), F32),
        ],
        scratch_shapes=[
            pltpu.SMEM(turn.shape, F32),
            pltpu.SMEM(shift.shape, F32),
            pltpu.SMEM(counts.shape, jnp.int32),
            pltpu.SMEM(ids.shape, jnp.int32),
            pltpu.VMEM(params.shape, F32),
            pltpu.VMEM(lists.shape, jnp.int32),
            pltpu.VMEM(goal.shape, F32),
            pltpu.VMEM(fetch.shape, jnp.int32),
            pltpu.VMEM((4, 2 * len(BY_MATRIX), HALF, WIDE), BF),
            pltpu.VMEM((4, len(BY_LANES), 2 * HALF, LANES), F32),
            blocks,
            blocks,
            pltpu.VMEM((18 * HALF, LANES), F32),
            pltpu.VMEM((entries, entries), BF),
            pltpu.VMEM((entries, entries), BF),
            pltpu.VMEM((9 * HALF, WIDE), F32),
            blocks,
            blocks,
            pltpu.VMEM((10 * HALF, WIDE), F32),
            pltpu.SemaphoreType.DMA((7,)),
            pltpu.SemaphoreType.DMA((3,)),
            pltpu.SemaphoreType.DMA((2,)),
            pltpu.SemaphoreType.DMA((3,)),
            pltpu.SemaphoreType.DMA((devices // 16,)),
        ],
        compiler_params=pltpu.CompilerParams(
            vmem_limit_bytes=52 << 20, collective_id=0, has_side_effects=True
        ),
        name="work",
    )(*[pltpu.with_memory_space_constraint(x, pltpu.HBM) for x in (turn, shift, counts, ids, fetch, params, lists, goal)])


def step_size(row):
    if row < 3:
        return 0.00016
    if row < 6:
        return 0.005
    if row < 10:
        return 0.001
    if row < 11:
        return 0.025
    if row < 14:
        return 0.0025
    return 0.000125


def adam_kernel(
    turn_hbm, shift_hbm, pulls_ref, painted_ref, params_ref, one_ref, two_ref,
    new_ref, new_one_ref, new_two_ref, image_ref, turn_ref, shift_ref, view_ref, load_sems,
):
    columns = params_ref.shape[1]
    total = params_ref.shape[0]
    rows = columns // LANES

    @pl.when(pl.program_id(0) == 0)
    def _():
        loads = [
            pltpu.make_async_copy(turn_hbm, turn_ref, load_sems.at[0]),
            pltpu.make_async_copy(shift_hbm, shift_ref, load_sems.at[1]),
        ]
        for load in loads:
            load.start()
        image_ref[...] = painted_ref[...]
        for load in loads:
            load.wait()
        for cam in range(4):
            matrix, eye = camera_of(turn_ref, shift_ref, cam, (rows, LANES))
            for k, value in enumerate(matrix[0] + matrix[1] + matrix[2] + eye):
                view_ref[cam, k] = value

    params = dense_rows(params_ref, columns)
    viewer = pulls_ref[9]
    view = [view_ref[0, k] for k in range(12)]
    for cam in range(1, 4):
        here = viewer > cam - 0.5
        view = [jnp.where(here, view_ref[cam, k], view[k]) for k in range(12)]
    matrix = [view[0:3], view[3:6], view[6:9]]
    eye = view[9:12]
    _, pull_back = jax.vjp(lambda *values: project(values, matrix, eye), *params)
    grads = list(pull_back([pulls_ref[r] for r in range(8)]))
    grads[10] = pulls_ref[8] * jax.nn.sigmoid(-params[10])
    for start in range(0, total, 8):
        size = min(8, total - start)
        gradient = jnp.stack(grads[start : start + size], axis=0).reshape(size, columns)
        at = pl.ds(start, size)
        new_one = BETA_ONE * one_ref[at, :] + (1.0 - BETA_ONE) * gradient
        new_two = BETA_TWO * two_ref[at, :] + (1.0 - BETA_TWO) * gradient * gradient
        sizes = [step_size(row) / BIAS_ONE for row in range(start, start + size)]
        rate = jnp.full((size, 1), sizes[0], F32)
        which = lax.broadcasted_iota(jnp.int32, (size, 1), 0)
        for k in range(1, size):
            if sizes[k] != sizes[k - 1]:
                rate = jnp.where(which >= k, sizes[k], rate)
        new_one_ref[at, :] = new_one
        new_two_ref[at, :] = new_two
        root = lax.rsqrt(new_two * (1.0 / BIAS_TWO))
        new_ref[at, :] = params_ref[at, :] - (rate * new_one) * (root * (1.0 - ADAM_EPS * root))


def apply_adam(pulls, painted, params, one, two, camera_turn, camera_shift):
    rows_in, own_count = params.shape
    columns = 4096
    block = pl.BlockSpec((rows_in, columns), lambda i: (0, i))
    return pl.pallas_call(
        adam_kernel,
        grid=(own_count // columns,),
        in_specs=[
            pl.BlockSpec(memory_space=pltpu.HBM),
            pl.BlockSpec(memory_space=pltpu.HBM),
            pl.BlockSpec((10, columns // LANES, LANES), lambda i: (0, i, 0)),
            pl.BlockSpec(memory_space=pltpu.VMEM),
            block,
            block,
            block,
        ],
        out_specs=[block] * 3 + [pl.BlockSpec(painted.shape, lambda i: (0, 0, 0))],
        out_shape=[jax.ShapeDtypeStruct(params.shape, F32)] * 3 + [jax.ShapeDtypeStruct(painted.shape, F32)],
        scratch_shapes=[
            pltpu.SMEM(camera_turn.shape, F32),
            pltpu.SMEM(camera_shift.shape, F32),
            pltpu.VMEM((4, 12, columns // LANES, LANES), F32),
            pltpu.SemaphoreType.DMA((2,)),
        ],
        compiler_params=pltpu.CompilerParams(vmem_limit_bytes=48 << 20),
        name="apply_adam",
    )(camera_turn, camera_shift, pulls, painted, params, one, two)


def shards(
    splat_params,
    first_moment,
    second_moment,
    camera_turn,
    camera_shift,
    fetch_table,
    tile_lists,
    tile_counts,
    tile_ids,
    target_image,
):
    devices, capacity = fetch_table.shape[1:]
    mesh_shape = (lax.axis_size("cam"), lax.axis_size("tile"))
    painted, pulls = work(
        mesh_shape,
        camera_turn,
        camera_shift,
        tile_counts,
        tile_ids,
        fetch_table.reshape(devices, 1, capacity),
        splat_params,
        tile_lists[0],
        target_image[:, 0],
    )
    updated_params, updated_first, updated_second, rendered = apply_adam(
        pulls, painted, splat_params, first_moment, second_moment, camera_turn, camera_shift
    )
    return (updated_params, updated_first, updated_second, rendered[:, None])


def solution(mesh):
    return jax.shard_map(
        shards,
        mesh=mesh,
        in_specs=(
            P(None, ("cam", "tile")),
            P(None, ("cam", "tile")),
            P(None, ("cam", "tile")),
            P(),
            P(),
            P(("cam", "tile"), None, None),
            P("cam", "tile", None),
            P("cam", "tile"),
            P("cam", "tile"),
            P(None, "cam", "tile", None),
        ),
        out_specs=(
            P(None, ("cam", "tile")),
            P(None, ("cam", "tile")),
            P(None, ("cam", "tile")),
            P(None, "cam", "tile", None),
        ),
        check_vma=False,
    )
```

```python
import functools
import math

import jax
import jax.numpy as jnp
from jax import lax
from jax.experimental import pallas as pl
from jax.experimental.pallas import tpu as pltpu
from jax.sharding import PartitionSpec as P

TILE_PX = 16
GRID = 32


FOCAL = 512.0
CENTRE = 256.0
EYE_GAP = 20.0
DILATION = 0.3
SH_ZERO = 0.28209479177387814
SH_ONE = 0.4886025119029199
SH_TWO = (
    1.0925484305920792,
    -1.0925484305920792,
    0.31539156525252005,
    -1.0925484305920792,
    0.5462742152960396,
)
SH_THREE = (
    -0.5900435899266435,
    2.890611442640554,
    -0.4570457994644658,
    0.3731763325901154,
    -0.4570457994644658,
    1.445305721320277,
    -0.5900435899266435,
)
BETA_ONE = 0.9
BETA_TWO = 0.999
BIAS_ONE = 1.0 - math.exp(2000.0 * math.log(0.9))
BIAS_TWO = 1.0 - math.exp(2000.0 * math.log(0.999))
ADAM_EPS = 1e-08


def harmonics(dir_x, dir_y, dir_z):
    sq_x = dir_x * dir_x
    sq_y = dir_y * dir_y
    sq_z = dir_z * dir_z
    return [
        SH_ZERO * jnp.ones_like(dir_x),
        -SH_ONE * dir_y,
        SH_ONE * dir_z,
        -SH_ONE * dir_x,
        SH_TWO[0] * dir_x * dir_y,
        SH_TWO[1] * dir_y * dir_z,
        SH_TWO[2] * (2.0 * sq_z - sq_x - sq_y),
        SH_TWO[3] * dir_x * dir_z,
        SH_TWO[4] * (sq_x - sq_y),
        SH_THREE[0] * dir_y * (3.0 * sq_x - sq_y),
        SH_THREE[1] * dir_x * dir_y * dir_z,
        SH_THREE[2] * dir_y * (4.0 * sq_z - sq_x - sq_y),
        SH_THREE[3] * dir_z * (2.0 * sq_z - 3.0 * sq_x - 3.0 * sq_y),
        SH_THREE[4] * dir_x * (4.0 * sq_z - sq_x - sq_y),
        SH_THREE[5] * dir_z * (sq_x - sq_y),
        SH_THREE[6] * dir_x * (sq_x - 3.0 * sq_y),
    ]


def quat_matrix(quat_w, quat_x, quat_y, quat_z):
    return [
        [
            1.0 - 2.0 * (quat_y * quat_y + quat_z * quat_z),
            2.0 * (quat_x * quat_y - quat_w * quat_z),
            2.0 * (quat_x * quat_z + quat_w * quat_y),
        ],
        [
            2.0 * (quat_x * quat_y + quat_w * quat_z),
            1.0 - 2.0 * (quat_x * quat_x + quat_z * quat_z),
            2.0 * (quat_y * quat_z - quat_w * quat_x),
        ],
        [
            2.0 * (quat_x * quat_z - quat_w * quat_y),
            2.0 * (quat_y * quat_z + quat_w * quat_x),
            1.0 - 2.0 * (quat_x * quat_x + quat_y * quat_y),
        ],
    ]

LOG2E = math.log2(math.e)
HALF = 64
WIDE = 256
LANES = 128
BIG = 3e38
BY_LANES = (0, 1, 8)
BY_MATRIX = (2, 3, 4, 5, 6, 7)
DEAD = -1e4
KEEP_MIN = 2.0**-24
EARLY_STEPS = 2
BF = jnp.bfloat16
F32 = jnp.float32


@jax.custom_vjp
def inverse(value):
    return 1.0 / value


def inverse_fwd(value):
    result = 1.0 / value
    return result, result


def inverse_bwd(result, pull):
    return (-pull * result * result,)


inverse.defvjp(inverse_fwd, inverse_bwd)


@jax.custom_vjp
def inverse_root(value):
    return 1.0 / jnp.sqrt(value)


def inverse_root_fwd(value):
    result = 1.0 / jnp.sqrt(value)
    return result, result


def inverse_root_bwd(result, pull):
    return (-0.5 * pull * result * (result * result),)


inverse_root.defvjp(inverse_root_fwd, inverse_root_bwd)


def project(params, camera, eye_pos):
    scales = [jnp.exp(params[3 + i]) for i in range(3)]
    inv_norm = inverse_root(
        params[6] * params[6]
        + params[7] * params[7]
        + params[8] * params[8]
        + params[9] * params[9]
    )
    rotation = quat_matrix(
        params[6] * inv_norm, params[7] * inv_norm, params[8] * inv_norm, params[9] * inv_norm
    )
    relative = [params[i] - eye_pos[i] for i in range(3)]
    in_view = [
        camera[i][0] * relative[0] + camera[i][1] * relative[1] + camera[i][2] * relative[2]
        for i in range(3)
    ]
    inv_depth = inverse(in_view[2])
    screen_x = FOCAL * in_view[0] * inv_depth + CENTRE
    screen_y = FOCAL * in_view[1] * inv_depth + CENTRE
    axes_cam = [
        [
            (
                camera[i][0] * rotation[0][k]
                + camera[i][1] * rotation[1][k]
                + camera[i][2] * rotation[2][k]
            )
            * scales[k]
            for k in range(3)
        ]
        for i in range(3)
    ]
    slope_x = FOCAL * in_view[0] * inv_depth * inv_depth
    slope_y = FOCAL * in_view[1] * inv_depth * inv_depth
    row_x = [FOCAL * inv_depth * axes_cam[0][k] - slope_x * axes_cam[2][k] for k in range(3)]
    row_y = [FOCAL * inv_depth * axes_cam[1][k] - slope_y * axes_cam[2][k] for k in range(3)]
    cov_xx = row_x[0] * row_x[0] + row_x[1] * row_x[1] + row_x[2] * row_x[2] + DILATION
    cov_xy = row_x[0] * row_y[0] + row_x[1] * row_y[1] + row_x[2] * row_y[2]
    cov_yy = row_y[0] * row_y[0] + row_y[1] * row_y[1] + row_y[2] * row_y[2] + DILATION
    inv_det = inverse(cov_xx * cov_yy - cov_xy * cov_xy)
    inv_dist = inverse_root(
        relative[0] * relative[0] + relative[1] * relative[1] + relative[2] * relative[2]
    )
    basis = harmonics(relative[0] * inv_dist, relative[1] * inv_dist, relative[2] * inv_dist)
    colours = []
    for channel in range(3):
        total = basis[0] * params[11 + channel]
        for k in range(1, 16):
            total = total + basis[k] * params[11 + 3 * k + channel]
        colours.append(jnp.maximum(total + 0.5, 0.0))
    return [
        screen_x,
        screen_y,
        cov_yy * inv_det,
        -cov_xy * inv_det,
        cov_xx * inv_det,
        colours[0],
        colours[1],
        colours[2],
    ]


def camera_of(turn_ref, shift_ref, cam, shape):
    turn = [jnp.full(shape, turn_ref[cam, i], F32) for i in range(3)]
    norm = jnp.sqrt(1.0 + (turn[0] * turn[0] + turn[1] * turn[1] + turn[2] * turn[2]))
    matrix = quat_matrix(1.0 / norm, turn[0] / norm, turn[1] / norm, turn[2] / norm)
    eye = [jnp.full(shape, shift_ref[cam, i], F32) for i in range(3)]
    eye[0] = EYE_GAP * cam + eye[0]
    return matrix, eye


def dense_rows(ref, columns):
    rows = []
    total = ref.shape[0]
    for start in range(0, total, 8):
        size = min(8, total - start)
        block = ref[start : start + size, :].reshape(size, columns // LANES, LANES)
        rows.extend(block[r] for r in range(size))
    return rows


def two_parts(value):
    high = value.astype(BF)
    return high, (value - high.astype(F32)).astype(BF)


def nt_dot(lhs, rhs):
    return lax.dot_general(lhs, rhs, (((1,), (1,)), ((), ())), preferred_element_type=F32)


def tn_dot(lhs, rhs):
    return lax.dot_general(lhs, rhs, (((0,), (0,)), ((), ())), preferred_element_type=F32)


def nn_dot(lhs, rhs):
    return lax.dot_general(lhs, rhs, (((1,), (0,)), ((), ())), preferred_element_type=F32)


def one_hots(index):
    count = index.shape[1]
    wide = ((index >> 13) * LANES + (index & 127)).astype(F32).astype(BF)
    narrow = ((index >> 7) & 63).astype(F32)
    one = jnp.ones((), BF)
    zero = jnp.zeros((), BF)
    rows = lax.broadcasted_iota(jnp.int32, (WIDE, count), 0).astype(F32).astype(BF)
    pick = jnp.where(rows == wide, one, zero)
    few = lax.broadcasted_iota(jnp.int32, (HALF, count), 0).astype(F32)
    return pick, jnp.where(few == narrow, 1.0, 0.0)


def matrix_pick(table, rows, index):
    pick, mask = one_hots(index)
    spread = nn_dot(table, pick)
    low = rows * HALF
    return [
        jnp.sum(
            (spread[r * HALF : (r + 1) * HALF] + spread[low + r * HALF : low + (r + 1) * HALF]) * mask,
            axis=0,
            keepdims=True,
        )
        for r in range(rows)
    ]


def lane_pick(loads, blocks, index):
    lanes = jnp.broadcast_to(index & 127, (8, LANES))
    level = index >> 10
    spot = lax.broadcasted_iota(jnp.int32, (8, LANES), 0) == ((index >> 7) & 7)
    bits = []
    while 2 ** len(bits) < blocks:
        bits.append(jnp.broadcast_to((level & 2 ** len(bits)) != 0, (8, LANES)))

    def tree(load, first, depth):
        if depth == 0:
            return jnp.take_along_axis(load(first), lanes, axis=1, mode="promise_in_bounds")
        half = 2 ** (depth - 1)
        return jnp.where(
            bits[depth - 1], tree(load, first + half, depth - 1), tree(load, first, depth - 1)
        )

    return [
        jnp.sum(jnp.where(spot, tree(load, 0, len(bits)), 0.0), axis=0, keepdims=True) for load in loads
    ]


def put_into(rows, index):
    pick, mask = one_hots(index)
    mask = mask.astype(BF)
    parts = [two_parts(row) for row in rows]
    placed = nt_dot(jnp.concatenate([mask * part[k] for k in range(2) for part in parts], axis=0), pick)
    low = len(rows) * HALF
    return placed[:low] + placed[low:]


MESH = pl.DeviceIdType.MESH


def signal_all(barrier, cams, tiles):
    own_cam = lax.axis_index("cam")
    own_tile = lax.axis_index("tile")
    for step in range(cams):
        cam = lax.rem(own_cam + step, cams)

        def tell(i, carry, cam=cam):
            pl.semaphore_signal(
                barrier, inc=1, device_id=(cam, lax.rem(own_tile + i, tiles)), device_id_type=MESH
            )
            return carry

        lax.fori_loop(1 if step == 0 else 0, tiles, tell, 0, unroll=4)


def project_block(turn_ref, shift_ref, params_ref, table_ref, exact_ref, half, step, columns):
    rows = columns // LANES
    start = pl.multiple_of(half * (HALF * LANES) + step * columns, columns)
    params = []
    total = params_ref.shape[0]
    for first in range(0, total, 8):
        size = min(8, total - first)
        block = params_ref[first : first + size, pl.ds(start, columns)].reshape(size, rows, LANES)
        params.extend(block[r] for r in range(size))
    opacity = jax.nn.sigmoid(params[10])
    at = half * LANES
    place = pl.ds(pl.multiple_of(step * rows, rows), rows)
    far = pl.ds(pl.multiple_of(half * HALF + step * rows, rows), rows)
    for cam in range(4):
        matrix, eye = camera_of(turn_ref, shift_ref, cam, (rows, LANES))
        record = project(params, matrix, eye) + [opacity]
        for r, value in enumerate(record):
            if r in BY_LANES:
                exact_ref[cam, BY_LANES.index(r), far, :] = value
            else:
                value = jnp.where(value == value, jnp.clip(value, -BIG, BIG), 0.0)
                for k, part in enumerate(two_parts(value)):
                    table_ref[cam, k * len(BY_MATRIX) + BY_MATRIX.index(r), place, at : at + LANES] = part


def ask_phase(cams, tiles, turn_ref, shift_ref, fetch_ref, params_ref, wanted_ref, table_ref, exact_ref,
              ready, send_sem, recv_sem, own_sem):
    columns = 2048
    steps = HALF * LANES // columns
    barrier = pltpu.get_barrier_semaphore()
    signal_all(barrier, cams, tiles)
    own_cam = lax.axis_index("cam")
    own_tile = lax.axis_index("tile")
    me = own_cam * tiles + own_tile
    others = cams * tiles - 1
    own = pltpu.make_async_copy(fetch_ref.at[me], wanted_ref.at[me], own_sem)
    own.start()
    for copy in ready:
        copy.wait()

    def body(step, carry):
        for half in range(2):
            project_block(turn_ref, shift_ref, params_ref, table_ref, exact_ref, half, step, columns)
        return carry

    early = EARLY_STEPS
    lax.fori_loop(0, early, body, 0)
    pl.semaphore_wait(barrier, others)
    for hop in range(cams):
        cam = lax.rem(own_cam + hop, cams)

        def ask(i, carry, cam=cam):
            tile = lax.rem(own_tile + i, tiles)
            pltpu.make_async_remote_copy(
                src_ref=fetch_ref.at[cam * tiles + tile],
                dst_ref=wanted_ref.at[me],
                send_sem=send_sem,
                recv_sem=recv_sem,
                device_id=(cam, tile),
                device_id_type=MESH,
            ).start()
            return carry

        lax.fori_loop(1 if hop == 0 else 0, tiles, ask, 0, unroll=4)
    lax.fori_loop(early, steps, body, 0)
    own.wait()
    many = pl.ds(0, others)
    pltpu.make_async_copy(fetch_ref.at[many], wanted_ref.at[many], send_sem).wait()
    pltpu.make_async_copy(fetch_ref.at[many], wanted_ref.at[many], recv_sem).wait()


def pair_of(ref, chip):
    return jnp.concatenate([ref[2 * chip], ref[2 * chip + 1]], axis=1)


def answer_phase(cams, tiles, wanted_ref, table_ref, exact_ref, got_ref, held_ref, send_sem, recv_sem, own_sem):
    chips = cams * tiles // 2
    per_cam = chips // cams
    others = 2 * chips - 1
    me = lax.axis_index("cam") * tiles + lax.axis_index("tile")
    own_chip = me // 2
    twin = 2 * own_chip + (1 - lax.rem(me, 2))

    def fill(chip):
        cam = chip // per_cam
        loads = [lambda v, r=r: exact_ref[cam, r, 8 * v : 8 * v + 8, :] for r in range(len(BY_LANES))]
        count = len(BY_MATRIX)
        middle = matrix_pick(
            table_ref[cam].reshape(2 * count * HALF, WIDE), count, pair_of(wanted_ref, chip)
        )
        for k in range(2):
            ends = lane_pick(loads, 2 * HALF // 8, wanted_ref[2 * chip + k])
            rows = [part[:, k * LANES : (k + 1) * LANES] for part in middle]
            held_ref[2 * chip + k, 0:9, :] = jnp.concatenate(ends[:2] + rows + ends[2:], axis=0)

    def send(other):
        pltpu.make_async_remote_copy(
            src_ref=held_ref.at[other, 0:9],
            dst_ref=got_ref.at[me, 0:9],
            send_sem=send_sem,
            recv_sem=recv_sem,
            device_id=(other // tiles, lax.rem(other, tiles)),
            device_id_type=MESH,
        ).start()

    per_batch = 8

    def fill_batch(batch):
        for k in range(per_batch):
            fill(lax.rem(own_chip + batch * per_batch + k, chips))

    def send_chip(step):
        chip = lax.rem(own_chip + step, chips)
        send(2 * chip)
        send(2 * chip + 1)

    fill_batch(0)
    own = pltpu.make_async_copy(held_ref.at[me, 0:9], got_ref.at[me, 0:9], own_sem)
    own.start()
    send(twin)
    for k in range(1, per_batch):
        send_chip(k)

    def body(batch, carry):
        fill_batch(batch)
        for k in range(per_batch):
            send_chip(batch * per_batch + k)
        return carry

    lax.fori_loop(1, chips // per_batch, body, 0)
    own.wait()
    many = pl.ds(0, others)
    pltpu.make_async_copy(held_ref.at[many, 0:9], got_ref.at[many, 0:9], send_sem).wait()
    pltpu.make_async_copy(held_ref.at[many, 0:9], got_ref.at[many, 0:9], recv_sem).wait()


def render_phase(
    counts_ref, ids_ref, got_ref, lists_ref, goal_ref, image_ref, grads_ref,
    table_ref, before_ref, after_ref, total_ref,
):
    tiles, entries = lists_ref.shape
    pixels = goal_ref.shape[2]

    for r in range(9):
        for i in range(0, 2 * HALF, 8):
            table_ref[r * 2 * HALF + i : r * 2 * HALF + i + 8, :] = jnp.concatenate([got_ref[i + k, r : r + 1, :] for k in range(8)], axis=0)
    row = lax.broadcasted_iota(jnp.int32, (entries, entries), 0) & 127
    col = lax.broadcasted_iota(jnp.int32, (entries, entries), 1)
    before_ref[...] = jnp.where(row < col, 1.0, 0.0).astype(BF)
    after_ref[...] = jnp.where((row > col) | (col >= LANES), 1.0, 0.0).astype(BF)
    total_ref[...] = jnp.zeros_like(total_ref)

    def opening(tile):
        index = lists_ref[pl.ds(tile, 1), :]
        live = lax.broadcasted_iota(jnp.int32, (1, entries), 1) < counts_ref[0, tile]
        number = ids_ref[0, tile]
        origin_x = ((number & 31) * TILE_PX + TILE_PX // 2).astype(F32)
        origin_y = ((number >> 5) * TILE_PX + TILE_PX // 2).astype(F32)
        loads = [
            lambda v, r=r: table_ref[r * 2 * HALF + 8 * v : r * 2 * HALF + 8 * v + 8, :] for r in range(9)
        ]
        left = lane_pick(loads, 2 * HALF // 8, index[:, :LANES])
        right = lane_pick(loads, 2 * HALF // 8, index[:, LANES:])
        rec = [jnp.concatenate([left[r], right[r]], axis=1) for r in range(9)]
        rec_u = jnp.where(live, rec[0] - origin_x, 0.0)
        rec_v = jnp.where(live, rec[1] - origin_y, 0.0)
        con_a = jnp.where(live, rec[2], 0.0)
        con_b = jnp.where(live, rec[3], 0.0)
        con_c = jnp.where(live, rec[4], 0.0)
        log_o = jnp.where(live, jnp.maximum(jnp.log(rec[8]) * LOG2E, DEAD), DEAD)
        colours = [jnp.where(live, c, 0.0) for c in rec[5:8]]

        spot = lax.broadcasted_iota(jnp.int32, (TILE_PX, entries), 0).astype(F32) - 7.5
        off_x = spot - rec_u
        off_y = spot - rec_v
        part_x = (-0.5 * LOG2E) * con_a * off_x * off_x + log_o
        cross = (-LOG2E) * con_b * off_x
        part_y = (-0.5 * LOG2E) * con_c * off_y * off_y
        power = jnp.concatenate(
            [part_x + (cross * off_y[y : y + 1] + part_y[y : y + 1]) for y in range(TILE_PX)], axis=0
        )
        alphas = jnp.exp2(power)
        log_keep = jnp.log(jnp.maximum(1.0 - alphas, KEEP_MIN))
        return index, rec_u, rec_v, con_a, con_b, con_c, colours, power, alphas, log_keep

    def running(values, mask):
        parts = [two_parts(value) for value in values]
        sides = (slice(0, LANES), slice(LANES, 2 * LANES))
        stacked = [
            jnp.concatenate([part[0][:, side], part[1][:, side]], axis=1) for part in parts for side in sides
        ]
        sums = nn_dot(jnp.concatenate(stacked, axis=0), mask)
        rows = values[0].shape[0]
        return [
            [sums[(2 * t + h) * rows : (2 * t + h + 1) * rows] for h in range(2)] for t in range(len(values))
        ]

    def painting(tile, colours, ahead, alphas):
        weights = jnp.exp(ahead) * alphas
        w_high, w_low = two_parts(weights)

        col_parts = [two_parts(c) for c in colours]
        col_high = [p[0].astype(F32) for p in col_parts]
        col_low = [p[1].astype(F32) for p in col_parts]
        empty = [jnp.zeros((1, entries), F32)]
        col_stack = jnp.concatenate(col_high + col_low + empty * 10, axis=0).astype(BF)
        first = nt_dot(col_stack, w_high)
        second = nt_dot(col_stack, w_low)
        painted = [first[c : c + 1] + (first[3 + c : 4 + c] + second[c : c + 1]) for c in range(3)]
        residual = []
        for c in range(3):
            image_ref[c, pl.ds(tile, 1), :] = painted[c]
            residual.append(painted[c] - goal_ref[c, pl.ds(tile, 1), :])
        res_parts = [two_parts(c) for c in residual]
        res_high = [p[0].astype(F32) for p in res_parts]
        res_low = [p[1].astype(F32) for p in res_parts]
        blank = [jnp.zeros((1, pixels), F32)]
        res_left = jnp.concatenate(res_high + res_high + res_low + blank * 7, axis=0).astype(BF)
        col_right = jnp.concatenate(col_high + col_low + col_high + empty * 7, axis=0).astype(BF)
        weight_pull = tn_dot(res_left, col_right)
        res_stack = jnp.concatenate(res_high + res_low + blank * 10, axis=0).astype(BF)
        pull_one = nn_dot(res_stack, w_high)
        pull_two = nn_dot(res_stack, w_low)
        col_grads = [
            pull_one[c : c + 1] + (pull_one[3 + c : 4 + c] + pull_two[c : c + 1]) for c in range(3)
        ]
        share = weight_pull * weights
        return share, weights, col_grads

    def closing(tile, index, rec_u, rec_v, con_a, con_b, con_c, power, log_keep, share, behind, col_grads):
        spot = lax.broadcasted_iota(jnp.int32, (TILE_PX, entries), 0).astype(F32) - 7.5
        odds = jnp.exp2(power - log_keep * LOG2E)
        pull = share - odds * behind

        sum0 = jnp.zeros((TILE_PX, entries), F32)
        sum1 = sum0
        sum2 = sum0
        for y in range(TILE_PX - 1, -1, -1):
            sum0 = sum0 + pull[y * TILE_PX : (y + 1) * TILE_PX]
            sum1 = sum1 + sum0
            sum2 = sum2 + sum1
        first_y = sum1 - 8.5 * sum0
        second_y = 2.0 * sum2 - 18.0 * sum1 + 72.25 * sum0

        def over_x(value):
            return jnp.sum(value, axis=0, keepdims=True)

        m00 = over_x(sum0)
        m10 = over_x(spot * sum0)
        m20 = over_x(spot * spot * sum0)
        m01 = over_x(first_y)
        m11 = over_x(spot * first_y)
        m02 = over_x(second_y)
        by_x = m10 - rec_u * m00
        by_y = m01 - rec_v * m00
        by_xx = m20 - rec_u * (2.0 * m10 - rec_u * m00)
        by_xy = m11 - rec_u * m01 - rec_v * (m10 - rec_u * m00)
        by_yy = m02 - rec_v * (2.0 * m01 - rec_v * m00)
        grads = [
            con_a * by_x + con_b * by_y,
            con_c * by_y + con_b * by_x,
            -0.5 * by_xx,
            -by_xy,
            -0.5 * by_yy,
            col_grads[0],
            col_grads[1],
            col_grads[2],
            m00,
        ]
        total_ref[...] += put_into(grads, index)

    def tile_step(group):
        opened = [opening(tile) for tile in group]
        sums = running([o[9] for o in opened], before_ref[...])
        aheads = [
            jnp.concatenate([left[:, :LANES], right[:, :LANES] + left[:, LANES:]], axis=1)
            for left, right in sums
        ]
        painted = [painting(t, o[6], a, o[8]) for t, o, a in zip(group, opened, aheads)]
        sums = running([p[0] for p in painted], after_ref[...])
        behinds = [
            jnp.concatenate([left[:, :LANES] + right[:, LANES:], right[:, :LANES]], axis=1)
            for left, right in sums
        ]
        for t, o, p, b in zip(group, opened, painted, behinds):
            closing(t, *o[:6], o[7], o[9], p[0], b, p[2])

    per_step = 16

    def body(step, carry):
        tile_step([step * per_step + k for k in range(per_step)])
        return carry

    lax.fori_loop(0, tiles // per_step, body, 0)
    def lay(step, carry):
        start = pl.multiple_of(8 * step, 8)
        for h in range(2):
            block = [
                total_ref[pl.ds(pl.multiple_of(r * HALF + start, 8), 8), h * LANES : (h + 1) * LANES]
                for r in range(9)
            ]
            for k in range(8):
                grads_ref[h * HALF + start + k, 0:9, :] = jnp.concatenate(
                    [part[k : k + 1] for part in block], axis=0
                )
        return carry

    lax.fori_loop(0, HALF // 8, lay, 0)


def collect_phase(
    cams, tiles, wanted_ref, away_ref, out_ref, back_ref, total_ref, send_sem, recv_sem, own_sem
):
    chips = cams * tiles // 2
    per_cam = chips // cams
    per_group = 8
    groups = chips // per_group
    ahead = 2
    others = 2 * chips - 1
    me = lax.axis_index("cam") * tiles + lax.axis_index("tile")
    own_chip = me // 2
    twin = 2 * own_chip + (1 - lax.rem(me, 2))
    own = pltpu.make_async_copy(away_ref.at[me, 0:9], back_ref.at[me, 0:9], own_sem)
    own.start()

    def send(other, group):
        pltpu.make_async_remote_copy(
            src_ref=away_ref.at[other, 0:9],
            dst_ref=back_ref.at[me, 0:9],
            send_sem=send_sem,
            recv_sem=recv_sem.at[group],
            device_id=(other // tiles, lax.rem(other, tiles)),
            device_id_type=MESH,
        ).start()

    def send_group(group, first):
        for k in range(first, per_group):
            chip = lax.rem(own_chip + group * per_group + k, chips)
            send(2 * chip, group)
            send(2 * chip + 1, group)

    send(twin, 0)
    send_group(0, 1)
    for group in range(1, ahead):
        send_group(group, 0)
    total_ref[...] = jnp.zeros_like(total_ref)
    own.wait()

    def add_group(group):
        for k in range(per_group):
            chip = lax.rem(own_chip + chips - (group * per_group + k), chips)
            both = jnp.concatenate([back_ref[2 * chip, 0:9, :], back_ref[2 * chip + 1, 0:9, :]], axis=1)
            viewer = jnp.full((1, WIDE), chip // per_cam, jnp.int32).astype(F32)
            rows = [both[r : r + 1] for r in range(9)] + [viewer]
            total_ref[...] += put_into(rows, pair_of(wanted_ref, chip))

    def arrive(group, count):
        block = pl.ds(0, count)
        pltpu.make_async_copy(away_ref.at[block, 0:9], back_ref.at[block, 0:9], recv_sem.at[group]).wait()

    def take_and_send(group, carry):
        send_group(group + ahead, 0)
        arrive(group, 2 * per_group)
        add_group(group)
        return carry

    def take(group, carry):
        arrive(group, 2 * per_group)
        add_group(group)
        return carry

    arrive(0, 2 * per_group - 1)
    send_group(ahead, 0)
    add_group(0)
    lax.fori_loop(1, groups - ahead, take_and_send, 0)
    lax.fori_loop(groups - ahead, groups, take, 0)
    for r in range(10):
        for h in range(2):
            out_ref[r, h * HALF : (h + 1) * HALF, :] = total_ref[
                r * HALF : (r + 1) * HALF, h * LANES : (h + 1) * LANES
            ]
    many = pl.ds(0, others)
    pltpu.make_async_copy(away_ref.at[many, 0:9], back_ref.at[many, 0:9], send_sem).wait()


def work_kernel(
    cams, tiles, turn_hbm, shift_hbm, counts_hbm, ids_hbm, fetch_hbm, params_hbm, lists_hbm, goal_hbm,
    image_ref, pulls_ref,
    turn_ref, shift_ref, counts_ref, ids_ref, params_ref, lists_ref, goal_ref,
    wanted_ref, table_ref, exact_ref, held_ref, got_ref, spread_ref, before_ref, after_ref, slots_ref,
    away_ref, back_ref, total_ref, load_sems, send_sems, recv_sems, own_sems, group_sems,
):
    loads = [
        pltpu.make_async_copy(source, target, load_sems.at[k])
        for k, (source, target) in enumerate(
            [
                (params_hbm, params_ref),
                (turn_hbm, turn_ref),
                (shift_hbm, shift_ref),
                (counts_hbm, counts_ref),
                (ids_hbm, ids_ref),
                (lists_hbm, lists_ref),
                (goal_hbm, goal_ref),
            ]
        )
    ]
    for load in loads:
        load.start()
    ask_phase(
        cams, tiles, turn_ref, shift_ref, fetch_hbm, params_ref, wanted_ref, table_ref, exact_ref,
        loads[:3], send_sems.at[0], recv_sems.at[0], own_sems.at[0],
    )
    answer_phase(
        cams, tiles, wanted_ref, table_ref, exact_ref, got_ref, held_ref,
        send_sems.at[1], recv_sems.at[1], own_sems.at[1],
    )
    for load in loads[3:]:
        load.wait()
    render_phase(
        counts_ref, ids_ref, got_ref, lists_ref, goal_ref, image_ref, away_ref,
        spread_ref, before_ref, after_ref, slots_ref,
    )
    collect_phase(
        cams, tiles, wanted_ref, away_ref, pulls_ref, back_ref, total_ref,
        send_sems.at[2], group_sems, own_sems.at[2],
    )


def work(mesh_shape, turn, shift, counts, ids, fetch, params, lists, goal):
    devices, _, capacity = fetch.shape
    entries = lists.shape[1]
    hbm = pl.BlockSpec(memory_space=pltpu.HBM)
    vmem = pl.BlockSpec(memory_space=pltpu.VMEM)
    blocks = pltpu.VMEM((devices, 16, capacity), F32)
    return pl.pallas_call(
        functools.partial(work_kernel, *mesh_shape),
        in_specs=[hbm] * 8,
        out_specs=[vmem] * 2,
        out_shape=[
            jax.ShapeDtypeStruct(goal.shape, F32),
            jax.ShapeDtypeStruct((10, 2 * HALF, LANES), F32),
        ],
        scratch_shapes=[
            pltpu.SMEM(turn.shape, F32),
            pltpu.SMEM(shift.shape, F32),
            pltpu.SMEM(counts.shape, jnp.int32),
            pltpu.SMEM(ids.shape, jnp.int32),
            pltpu.VMEM(params.shape, F32),
            pltpu.VMEM(lists.shape, jnp.int32),
            pltpu.VMEM(goal.shape, F32),
            pltpu.VMEM(fetch.shape, jnp.int32),
            pltpu.VMEM((4, 2 * len(BY_MATRIX), HALF, WIDE), BF),
            pltpu.VMEM((4, len(BY_LANES), 2 * HALF, LANES), F32),
            blocks,
            blocks,
            pltpu.VMEM((18 * HALF, LANES), F32),
            pltpu.VMEM((entries, entries), BF),
            pltpu.VMEM((entries, entries), BF),
            pltpu.VMEM((9 * HALF, WIDE), F32),
            blocks,
            blocks,
            pltpu.VMEM((10 * HALF, WIDE), F32),
            pltpu.SemaphoreType.DMA((7,)),
            pltpu.SemaphoreType.DMA((3,)),
            pltpu.SemaphoreType.DMA((2,)),
            pltpu.SemaphoreType.DMA((3,)),
            pltpu.SemaphoreType.DMA((devices // 16,)),
        ],
        compiler_params=pltpu.CompilerParams(
            vmem_limit_bytes=52 << 20, collective_id=0, has_side_effects=True
        ),
        name="work",
    )(*[pltpu.with_memory_space_constraint(x, pltpu.HBM) for x in (turn, shift, counts, ids, fetch, params, lists, goal)])


def step_size(row):
    if row < 3:
        return 0.00016
    if row < 6:
        return 0.005
    if row < 10:
        return 0.001
    if row < 11:
        return 0.025
    if row < 14:
        return 0.0025
    return 0.000125


def adam_kernel(
    turn_hbm, shift_hbm, pulls_ref, painted_ref, params_ref, one_ref, two_ref,
    new_ref, new_one_ref, new_two_ref, image_ref, turn_ref, shift_ref, view_ref, load_sems,
):
    columns = params_ref.shape[1]
    total = params_ref.shape[0]
    rows = columns // LANES

    @pl.when(pl.program_id(0) == 0)
    def _():
        loads = [
            pltpu.make_async_copy(turn_hbm, turn_ref, load_sems.at[0]),
            pltpu.make_async_copy(shift_hbm, shift_ref, load_sems.at[1]),
        ]
        for load in loads:
            load.start()
        image_ref[...] = painted_ref[...]
        for load in loads:
            load.wait()
        for cam in range(4):
            matrix, eye = camera_of(turn_ref, shift_ref, cam, (rows, LANES))
            for k, value in enumerate(matrix[0] + matrix[1] + matrix[2] + eye):
                view_ref[cam, k] = value

    params = dense_rows(params_ref, columns)
    viewer = pulls_ref[9]
    view = [view_ref[0, k] for k in range(12)]
    for cam in range(1, 4):
        here = viewer > cam - 0.5
        view = [jnp.where(here, view_ref[cam, k], view[k]) for k in range(12)]
    matrix = [view[0:3], view[3:6], view[6:9]]
    eye = view[9:12]
    _, pull_back = jax.vjp(lambda *values: project(values, matrix, eye), *params)
    grads = list(pull_back([pulls_ref[r] for r in range(8)]))
    grads[10] = pulls_ref[8] * jax.nn.sigmoid(-params[10])
    for start in range(0, total, 8):
        size = min(8, total - start)
        gradient = jnp.stack(grads[start : start + size], axis=0).reshape(size, columns)
        at = pl.ds(start, size)
        new_one = BETA_ONE * one_ref[at, :] + (1.0 - BETA_ONE) * gradient
        new_two = BETA_TWO * two_ref[at, :] + (1.0 - BETA_TWO) * gradient * gradient
        sizes = [step_size(row) / BIAS_ONE for row in range(start, start + size)]
        rate = jnp.full((size, 1), sizes[0], F32)
        which = lax.broadcasted_iota(jnp.int32, (size, 1), 0)
        for k in range(1, size):
            if sizes[k] != sizes[k - 1]:
                rate = jnp.where(which >= k, sizes[k], rate)
        new_one_ref[at, :] = new_one
        new_two_ref[at, :] = new_two
        root = lax.rsqrt(new_two * (1.0 / BIAS_TWO))
        new_ref[at, :] = params_ref[at, :] - (rate * new_one) * (root * (1.0 - ADAM_EPS * root))


def apply_adam(pulls, painted, params, one, two, camera_turn, camera_shift):
    rows_in, own_count = params.shape
    columns = 4096
    block = pl.BlockSpec((rows_in, columns), lambda i: (0, i))
    return pl.pallas_call(
        adam_kernel,
        grid=(own_count // columns,),
        in_specs=[
            pl.BlockSpec(memory_space=pltpu.HBM),
            pl.BlockSpec(memory_space=pltpu.HBM),
            pl.BlockSpec((10, columns // LANES, LANES), lambda i: (0, i, 0)),
            pl.BlockSpec(memory_space=pltpu.VMEM),
            block,
            block,
            block,
        ],
        out_specs=[block] * 3 + [pl.BlockSpec(painted.shape, lambda i: (0, 0, 0))],
        out_shape=[jax.ShapeDtypeStruct(params.shape, F32)] * 3 + [jax.ShapeDtypeStruct(painted.shape, F32)],
        scratch_shapes=[
            pltpu.SMEM(camera_turn.shape, F32),
            pltpu.SMEM(camera_shift.shape, F32),
            pltpu.VMEM((4, 12, columns // LANES, LANES), F32),
            pltpu.SemaphoreType.DMA((2,)),
        ],
        compiler_params=pltpu.CompilerParams(vmem_limit_bytes=48 << 20),
        name="apply_adam",
    )(camera_turn, camera_shift, pulls, painted, params, one, two)


def shards(
    splat_params,
    first_moment,
    second_moment,
    camera_turn,
    camera_shift,
    fetch_table,
    tile_lists,
    tile_counts,
    tile_ids,
    target_image,
):
    devices, capacity = fetch_table.shape[1:]
    mesh_shape = (lax.axis_size("cam"), lax.axis_size("tile"))
    painted, pulls = work(
        mesh_shape,
        camera_turn,
        camera_shift,
        tile_counts,
        tile_ids,
        fetch_table.reshape(devices, 1, capacity),
        splat_params,
        tile_lists[0],
        target_image[:, 0],
    )
    updated_params, updated_first, updated_second, rendered = apply_adam(
        pulls, painted, splat_params, first_moment, second_moment, camera_turn, camera_shift
    )
    return (updated_params, updated_first, updated_second, rendered[:, None])


def solution(mesh):
    return jax.shard_map(
        shards,
        mesh=mesh,
        in_specs=(
            P(None, ("cam", "tile")),
            P(None, ("cam", "tile")),
            P(None, ("cam", "tile")),
            P(),
            P(),
            P(("cam", "tile"), None, None),
            P("cam", "tile", None),
            P("cam", "tile"),
            P("cam", "tile"),
            P(None, "cam", "tile", None),
        ),
        out_specs=(
            P(None, ("cam", "tile")),
            P(None, ("cam", "tile")),
            P(None, ("cam", "tile")),
            P(None, "cam", "tile", None),
        ),
        check_vma=False,
    )
```
